32 devices in a mesh: groups: 2 (over y), probe: 4 (over z), depth: 2 (over x), tile: 2 (over core).
Axes of the slice: x: 2, y: 2, z: 4, core: 2. Of those that a mesh axis runs over, the one named last changes fastest.
Arguments:
- stored_waves: bfloat16 [2, 16, 2, 256, 256], P('depth', ('groups', 'probe', 'tile')), parts along dimension 1, may hold values from -6 to 6
- transmission: bfloat16 [2, 16, 2, 256, 256], P('depth', ('groups', 'probe', 'tile')), parts along dimension 1
- residual: float32 [16, 2, 256, 256], P(('groups', 'probe', 'tile')), parts along dimension 0, may hold values from -0.6 to 0.6
- offsets: int32 [16, 2], P('groups'), parts along dimension 0, may hold values from 0 to 256
- slot_position: int32 [16], P(('groups', 'probe', 'tile')), parts along dimension 0, may hold values from 0 to 7, each once
Outputs:
- object_gradient: float32 [4, 2, 512, 512], P('groups', 'depth', 'probe', 'tile'), parts along dimension 0
The draws below stay inside these ranges and needn't reach their ends.
There are 2 independent parts, one for each index of `groups`. The reference program is written for one: setup_inputs(seed, part) draws one part's arguments, and reference() takes and returns one part's arrays. A program takes and returns all parts, laid end to end along the dimension named above; each array names one. Nothing has to cross between parts.
Inputs may be any that keep to these rules, and one draw needn't show every extreme that they name: `slot_position`: every scan position is held by exactly one slot.
All inputs are finite; a program needn't handle non-finite values.
Results may differ from the reference program's by a relative error of at most 0.0032.
Values may be sent and summed in bfloat16 or wider, within the bound.
A program may use at most 64 MiB of HBM per device.

```python
import math
import jax
import jax.numpy as jnp
from jax import lax

W = 256
OBJ = 512
SLICES = 2
POSITIONS = 8


def draw_transmission(key, part):
    amp_key, phase_key = jax.random.split(key)
    draw_shape = (SLICES, POSITIONS, 1, W, W)
    amplitude = jnp.exp(jax.random.uniform(amp_key, draw_shape, jnp.float32, math.log(0.75), 0.0))
    phase_angle = jax.random.uniform(phase_key, draw_shape, jnp.float32, -math.pi, math.pi)
    return jnp.concatenate([amplitude * jnp.cos(phase_angle), amplitude * jnp.sin(phase_angle)], axis=2).astype(jnp.bfloat16)


def set_ends(values, own_key, least, largest):
    place = [jax.random.randint(jax.random.fold_in(own_key, axis), (), 0, length) for axis, length in enumerate(values.shape)]
    main_axis = values.shape.index(max(values.shape))
    next_to = place[:main_axis] + [(place[main_axis] + 1) % values.shape[main_axis]] + place[main_axis + 1:]
    return values.at[tuple(place)].set(least).at[tuple(next_to)].set(largest)


def block_scale(stream_key, dims, cuts, smallest, top_value):
    def one(axis_at, shards_of):
        draws = jax.random.uniform(jax.random.fold_in(jax.random.fold_in(stream_key, 6), axis_at), (shards_of,), jnp.float32, smallest / len(cuts), top_value / len(cuts))
        return jnp.repeat(jnp.exp(draws), dims[axis_at] // shards_of).reshape((-1,) + (1,) * (len(dims) - axis_at - 1))

    level = one(*cuts[0])
    for cut in cuts[1:]:
        level = level * one(*cut)
    return level


def centred(rng, shape, scale, reach, cuts=(), kind=jnp.bfloat16):
    values = jax.random.normal(rng, shape, jnp.float32) * scale
    if len(cuts) > 0:
        values = block_scale(rng, shape, cuts, -0.22, 0.18) * values
    return jnp.clip(values, min=-reach, max=reach).astype(kind)


def setup_inputs(seed: int = 0, part: int = 0) -> dict:
    keys = jax.random.split(jax.random.key(seed), 6)
    own_keys = jax.random.split(jax.random.fold_in(keys[5], part), 6)
    stored_waves = centred(own_keys[0], (SLICES, POSITIONS, 2, W, W), 1.0, 6.0, ((0, 2), (1, 8)))
    transmission = draw_transmission(jax.random.fold_in(jax.random.fold_in(keys[5], part), 71), part)
    residual = centred(own_keys[2], (POSITIONS, 2, W, W), 0.1, 0.6, ((0, 8),), jnp.float32)
    offsets = set_ends(jax.random.randint(own_keys[3], (POSITIONS, 2), 0, OBJ - W + 1), jax.random.fold_in(own_keys[3], 1), 0, OBJ - W).astype(jnp.int32)
    slot_position = jax.random.permutation(own_keys[4], POSITIONS).astype(jnp.int32)
    return dict(stored_waves=stored_waves, transmission=transmission, residual=residual, offsets=offsets, slot_position=slot_position)


def back_propagate(field_real, field_imag):
    side_length = field_real.shape[-1]
    counter = jnp.arange(side_length, dtype=jnp.int32)
    frequency = ((counter + side_length // 2) % side_length - side_length // 2).astype(jnp.float32)
    phase_angle = 0.5 * (frequency[:, None] * frequency[:, None] + frequency[None, :] * frequency[None, :]) / side_length
    spectrum = jnp.fft.fft2(field_real + 1j * field_imag)
    spectrum = spectrum * (jnp.cos(phase_angle) + 1j * jnp.sin(phase_angle))
    result = jnp.fft.ifft2(spectrum)
    return jnp.real(result), jnp.imag(result)


def reference(stored_waves, transmission, residual, offsets, slot_position):
    slice_count = stored_waves.shape[0]
    positions = stored_waves.shape[1]
    side_length = stored_waves.shape[-1]
    corners = offsets[slot_position]
    adjoint_real = residual[:, 0]
    adjoint_imag = residual[:, 1]
    handed_real = adjoint_real
    handed_imag = adjoint_imag
    grads_real = []
    grads_imag = []
    for slice_number in range(slice_count - 1, -1, -1):
        if slice_number < slice_count - 1:
            adjoint_real, adjoint_imag = back_propagate(handed_real, handed_imag)
        wave_real = stored_waves[slice_number, :, 0].astype(jnp.float32)
        wave_imag = stored_waves[slice_number, :, 1].astype(jnp.float32)
        grads_real.insert(0, wave_real * adjoint_real + wave_imag * adjoint_imag)
        grads_imag.insert(0, wave_real * adjoint_imag - wave_imag * adjoint_real)
        trans_real = transmission[slice_number, :, 0].astype(jnp.float32)
        trans_imag = transmission[slice_number, :, 1].astype(jnp.float32)
        rounded = lax.optimization_barrier(((trans_real * adjoint_real + trans_imag * adjoint_imag).astype(jnp.bfloat16),
                                            (trans_real * adjoint_imag - trans_imag * adjoint_real).astype(jnp.bfloat16)))
        handed_real = rounded[0].astype(jnp.float32)
        handed_imag = rounded[1].astype(jnp.float32)
    gradient = jnp.stack([jnp.stack(grads_real), jnp.stack(grads_imag)])
    region = jnp.zeros((2, slice_count, OBJ, OBJ), jnp.float32)

    def add_patch(number, region):
        patch_value = lax.dynamic_index_in_dim(gradient, number, 2, keepdims=False)
        anchor = jnp.int32(0)
        corner = (anchor, anchor, corners[number, 0].astype(jnp.int32), corners[number, 1].astype(jnp.int32))
        current = lax.dynamic_slice(region, corner, (2, slice_count, side_length, side_length))
        return lax.dynamic_update_slice(region, current + patch_value, corner)

    return lax.fori_loop(0, positions, add_patch, region)
```

```python
import functools

import jax
import jax.numpy as jnp
import ml_dtypes
import numpy as np
from jax import lax
from jax.experimental import pallas as pl
from jax.experimental.pallas import tpu as pltpu
from jax.sharding import PartitionSpec as P

OBJ = 512
CHUNKS = 1
MESH = pl.DeviceIdType.MESH
F32 = jnp.float32
BF16 = jnp.bfloat16


def propagator(side):
    counter = np.arange(side)
    frequency = (counter + side // 2) % side - side // 2
    chirp = np.exp(0.5j * frequency.astype(np.float64) ** 2 / side)
    column = np.fft.ifft(chirp)
    matrix = column[(counter[:, None] - counter[None, :]) % side]
    parts = np.concatenate([matrix.real, matrix.imag], axis=1)
    high = parts.astype(ml_dtypes.bfloat16)
    low = (parts - high.astype(np.float64)).astype(ml_dtypes.bfloat16)
    return np.stack([high, low])


def dot(a, b):
    return jnp.dot(a, b, preferred_element_type=F32)


def split(value):
    high = value.astype(BF16)
    return high, (value - high.astype(F32)).astype(BF16)


def conj_times(layer_real, layer_imag, real, imag):
    return (
        layer_real * real + layer_imag * imag,
        layer_real * imag - layer_imag * real,
    )


def flip(index, mask, count):
    result, bit = 0, 1
    while bit < count:
        result = result + ((index // bit + (mask // bit) % 2) % 2) * bit
        bit *= 2
    return result


def kernel(
    depth_count,
    probe_count,
    waves_hbm,
    layers_hbm,
    residual_hbm,
    offsets,
    slot,
    table_hbm,
    out,
    waves,
    layers,
    residual,
    table,
    hand_out,
    hand_in,
    turned,
    grads,
    corners,
    direct_out,
    direct_in,
    pair_out,
    pair_in,
    sum_out,
    sum_in,
    held,
    load_sems,
    hand_sems,
    grad_sems,
    corner_sems,
    direct_sems,
    pair_sems,
    sum_sems,
):
    side = waves.shape[-1]
    rows, columns = out.shape[2], out.shape[3]
    step = side // CHUNKS
    depth = lax.axis_index("depth")
    probe = lax.axis_index("probe")
    tile = lax.axis_index("tile")
    is_top = depth == depth_count - 1
    has_below = depth > 0

    barrier = pltpu.get_barrier_semaphore()
    for mask in range(1, probe_count):
        pl.semaphore_signal(
            barrier, inc=1, device_id={"probe": flip(probe, mask, probe_count)}, device_id_type=MESH
        )
    pl.semaphore_signal(barrier, inc=1, device_id={"tile": 1 - tile}, device_id_type=MESH)

    @pl.when(depth < depth_count - 1)
    def _():
        pl.semaphore_signal(barrier, inc=1, device_id={"depth": depth + 1}, device_id_type=MESH)

    load_residual = pltpu.make_async_copy(residual_hbm, residual, load_sems.at[0])
    load_layers = pltpu.make_async_copy(layers_hbm, layers, load_sems.at[1])
    load_waves = pltpu.make_async_copy(waves_hbm, waves, load_sems.at[2])
    load_table = pltpu.make_async_copy(table_hbm, table, load_sems.at[3])

    @pl.when(is_top)
    def _():
        load_residual.start()

    if depth_count > 1:

        @pl.when(has_below)
        def _():
            load_layers.start()

        @pl.when(jnp.logical_not(is_top))
        def _():
            load_table.start()

    load_waves.start()

    own_slot = slot[0]
    top_row = offsets[0, own_slot]
    left_column = offsets[1, own_slot]
    corners[0, 0:8, :] = jnp.full((8, side), top_row, jnp.int32)
    corners[0, 8:16, :] = jnp.full((8, side), left_column, jnp.int32)

    @pl.when(has_below)
    def _():
        pl.semaphore_wait(barrier, probe_count + 1)

    @pl.when(jnp.logical_not(has_below))
    def _():
        pl.semaphore_wait(barrier, probe_count)

    corner_copy = pltpu.make_async_remote_copy(
        src_ref=corners.at[0],
        dst_ref=corners.at[1],
        send_sem=corner_sems.at[0],
        recv_sem=corner_sems.at[1],
        device_id={"tile": 1 - tile},
        device_id_type=MESH,
    )
    corner_copy.start()

    def hand_copy(part):
        window = pl.ds(part * step, step)
        return pltpu.make_async_remote_copy(
            src_ref=hand_out.at[:, window, :],
            dst_ref=hand_in.at[:, window, :],
            send_sem=hand_sems.at[0, part],
            recv_sem=hand_sems.at[1, part],
            device_id={"depth": depth - 1},
            device_id_type=MESH,
        )

    def grad_copy(part):
        window = pl.ds(part * step, step)
        return pltpu.make_async_remote_copy(
            src_ref=grads.at[0, :, window, :],
            dst_ref=grads.at[1, :, window, :],
            send_sem=grad_sems.at[0, part],
            recv_sem=grad_sems.at[1, part],
            device_id={"tile": 1 - tile},
            device_id_type=MESH,
        )

    def hand_down(part, real, imag):
        window = pl.ds(part * step, step)
        handed = conj_times(
            layers[0, 0, 0, window, :].astype(F32), layers[0, 0, 1, window, :].astype(F32), real, imag
        )
        hand_out[0, window, :] = handed[0].astype(BF16)
        hand_out[1, window, :] = handed[1].astype(BF16)
        hand_copy(part).start()

    def give_gradient(part, real, imag):
        window = pl.ds(part * step, step)
        gradient = conj_times(
            waves[0, 0, 0, window, :].astype(F32), waves[0, 0, 1, window, :].astype(F32), real, imag
        )
        grads[0, 0, window, :] = gradient[0].astype(BF16)
        grads[0, 1, window, :] = gradient[1].astype(BF16)
        grad_copy(part).start()

    @pl.when(is_top)
    def _():
        load_residual.wait()
        if depth_count > 1:
            load_layers.wait()
            for part in range(CHUNKS):
                window = pl.ds(part * step, step)
                hand_down(part, residual[0, 0, window, :], residual[0, 1, window, :])
        load_waves.wait()
        for part in range(CHUNKS):
            window = pl.ds(part * step, step)
            give_gradient(part, residual[0, 0, window, :], residual[0, 1, window, :])

    if depth_count > 1:

        @pl.when(jnp.logical_not(is_top))
        def _():
            load_table.wait()
            load_waves.wait()
            if depth_count > 2:

                @pl.when(has_below)
                def _():
                    load_layers.wait()

            for part in range(CHUNKS):
                window = pl.ds(part * step, step)
                hand_copy(part).wait_recv()
                real = dot(hand_in[0, window, :], table[0]) + dot(hand_in[0, window, :], table[1])
                imag = dot(hand_in[1, window, :], table[0]) + dot(hand_in[1, window, :], table[1])
                product = real[:, :side] - imag[:, side:], real[:, side:] + imag[:, :side]
                for c in range(2):
                    turned[window, pl.ds(c * side, side)] = product[c].astype(BF16)

            for part in range(CHUNKS):
                window = pl.ds(part * step, step)

                def from_left(index):
                    columns = pl.ds(index * side, side)
                    return (
                        dot(table[0, window, columns], turned[...]) + dot(table[1, window, columns], turned[...])
                    )

                by_real, by_imag = from_left(0), from_left(1)
                real = by_real[:, :side] - by_imag[:, side:]
                imag = by_real[:, side:] + by_imag[:, :side]
                if depth_count > 2:

                    @pl.when(has_below)
                    def _():
                        hand_down(part, real, imag)

                give_gradient(part, real, imag)

    row_index = lax.broadcasted_iota(jnp.int32, (side, columns), 0)
    column_index = lax.broadcasted_iota(jnp.int32, (side, columns), 1) + tile * columns

    def onehot(match):
        return jnp.where(match, 1.0, 0.0).astype(BF16)

    own_columns = onehot(column_index - row_index == left_column)
    placed = [[dot(grads[0, c], own_columns).astype(BF16)] for c in range(2)]

    corner_copy.wait_recv()
    for part in range(CHUNKS):
        grad_copy(part).wait_recv()
    peer_row = corners[1, 0:1, :]
    peer_columns = onehot(column_index - row_index == corners[1, 8:9, 0:columns])
    for c in range(2):
        placed[c].append(dot(grads[1, c], peer_columns).astype(BF16))

    strip_row = lax.broadcasted_iota(jnp.int32, (rows, side), 0)
    patch_row = lax.broadcasted_iota(jnp.int32, (rows, side), 1)
    distance = strip_row - patch_row

    def strip_part(owner, c):
        shifted = distance + owner * rows
        own_rows = onehot(shifted == top_row)
        peer_rows = onehot(shifted == peer_row)
        return dot(own_rows, placed[c][0]) + dot(peer_rows, placed[c][1])

    def strip(owner):
        return [strip_part(owner, c) for c in range(2)]

    def direct_copy(mask, c):
        place = mask - 1 if c == 0 else probe_count - 1
        return pltpu.make_async_remote_copy(
            src_ref=direct_out.at[place],
            dst_ref=direct_in.at[place],
            send_sem=direct_sems.at[0, place],
            recv_sem=direct_sems.at[1, place],
            device_id={"probe": flip(probe, mask, probe_count)},
            device_id_type=MESH,
        )

    def pair_copy(place):
        return pltpu.make_async_remote_copy(
            src_ref=pair_out.at[place],
            dst_ref=pair_in.at[place],
            send_sem=pair_sems.at[0, place],
            recv_sem=pair_sems.at[1, place],
            device_id={"probe": flip(probe, 1, probe_count)},
            device_id_type=MESH,
        )

    def sum_copy(place):
        return pltpu.make_async_remote_copy(
            src_ref=sum_out.at[place],
            dst_ref=sum_in.at[place],
            send_sem=sum_sems.at[0, place],
            recv_sem=sum_sems.at[1, place],
            device_id={"probe": flip(probe, 2 * place + 2, probe_count)},
            device_id_type=MESH,
        )

    others = range(probe_count // 2 - 1, 0, -1)
    for other in others:
        mask = 2 * other + 1
        owner = flip(probe, mask, probe_count)
        pair_out[other - 1] = strip_part(owner, 1).astype(BF16)
        pair_copy(other - 1).start()
        direct_out[mask - 1] = strip_part(owner, 0).astype(BF16)
        direct_copy(mask, 0).start()
    for other in others:
        mask = 2 * other
        real, imag = strip(flip(probe, mask, probe_count))
        direct_out[mask - 1] = real.astype(BF16)
        direct_copy(mask, 0).start()
        held[other - 1] = imag
    real, imag = strip(flip(probe, 1, probe_count))
    direct_out[0] = real.astype(BF16)
    direct_out[probe_count - 1] = imag.astype(BF16)
    direct_copy(1, 0).start()
    direct_copy(1, 1).start()
    for other in others:
        pair_copy(other - 1).wait_recv()
        sum_out[other - 1] = (held[other - 1] + pair_in[other - 1].astype(F32)).astype(BF16)
        sum_copy(other - 1).start()
    total = strip(probe)
    for c in range(2):
        out[c, 0] = total[c]
    for mask in range(probe_count - 1, 0, -1):
        direct_copy(mask, 0).wait_recv()
        out[0, 0] += direct_in[mask - 1].astype(F32)
    direct_copy(1, 1).wait_recv()
    out[1, 0] += direct_in[probe_count - 1].astype(F32)
    for other in others:
        sum_copy(other - 1).wait_recv()
        out[1, 0] += sum_in[other - 1].astype(F32)

    corner_copy.wait_send()
    for part in range(CHUNKS):
        grad_copy(part).wait_send()
    for mask in range(1, probe_count):
        direct_copy(mask, 0).wait_send()
    direct_copy(1, 1).wait_send()
    for other in others:
        pair_copy(other - 1).wait_send()
        sum_copy(other - 1).wait_send()

    @pl.when(has_below)
    def _():
        for part in range(CHUNKS):
            hand_copy(part).wait_send()


def rolled_kernel(
    chunks,
    pair_from,
    lag,
    waves_hbm,
    layers_hbm,
    residual_hbm,
    offsets_hbm,
    slot,
    table_hbm,
    out,
    waves,
    layers,
    residual,
    table,
    offsets,
    shifted,
    hand_out,
    hand_in,
    rolled,
    grads,
    masks,
    corners,
    far_out,
    far_in,
    mid_out,
    mid_in,
    near_out,
    near_in,
    pair_in,
    load_sems,
    hand_sems,
    grad_sems,
    corner_sems,
    far_sems,
    mid_sems,
    near_sems,
    pair_sems,
    sum_sems,
    ready_sems,
):
    side = waves.shape[-1]
    rows = out.shape[2]
    blocks = side // rows
    step = rows // chunks
    height = blocks * step
    depth = lax.axis_index("depth")
    probe = lax.axis_index("probe")
    tile = lax.axis_index("tile")
    is_top = depth == 1
    probe_count = 4

    barrier = pltpu.get_barrier_semaphore()
    pl.semaphore_signal(barrier, inc=1, device_id={"tile": 1 - tile}, device_id_type=MESH)

    @pl.when(jnp.logical_not(is_top))
    def _():
        pl.semaphore_signal(barrier, inc=1, device_id={"depth": 1, "tile": 0}, device_id_type=MESH)
        for mask in range(1, probe_count):
            pl.semaphore_signal(
                barrier, inc=1, device_id={"probe": flip(probe, mask, probe_count)}, device_id_type=MESH
            )

    @pl.when(is_top)
    def _():
        for mask in range(1, probe_count):
            pl.semaphore_signal(
                barrier,
                inc=1,
                device_id={"probe": flip(probe, mask, probe_count), "tile": 1},
                device_id_type=MESH,
            )

    load_offsets = pltpu.make_async_copy(offsets_hbm, offsets, load_sems.at[4])
    load_residual = pltpu.make_async_copy(residual_hbm, residual, load_sems.at[0])
    load_layers = pltpu.make_async_copy(layers_hbm, layers, load_sems.at[1])
    load_waves = pltpu.make_async_copy(waves_hbm, waves, load_sems.at[2])
    load_table = pltpu.make_async_copy(table_hbm, table, load_sems.at[3])
    load_offsets.start()
    load_table.start()

    @pl.when(is_top)
    def _():
        load_residual.start()
        load_layers.start()

    load_waves.start()

    load_offsets.wait()
    own_slot = slot[0]
    top_row = offsets[0, own_slot]
    left_column = offsets[1, own_slot]

    def onehot(match):
        return jnp.where(match, 1.0, 0.0).astype(BF16)

    row = lax.broadcasted_iota(jnp.int32, (side, side), 0)
    column = lax.broadcasted_iota(jnp.int32, (side, side), 1)
    canvas_row = (row % height) // step * rows + row // height * step + row % step
    row_move = onehot(column == (canvas_row - top_row) & (side - 1))
    column_move = onehot(row == (column - left_column) & (side - 1))

    def roll(value):
        return dot(dot(row_move, value).astype(BF16), column_move)

    def hand_copy(chunk):
        return pltpu.make_async_remote_copy(
            src_ref=hand_out.at[chunk],
            dst_ref=hand_in.at[chunk],
            send_sem=hand_sems.at[0, chunk],
            recv_sem=hand_sems.at[1, chunk],
            device_id={"depth": 0},
            device_id_type=MESH,
        )

    def grad_copy(chunk):
        return pltpu.make_async_remote_copy(
            src_ref=grads.at[0, chunk],
            dst_ref=grads.at[1, chunk],
            send_sem=grad_sems.at[0, chunk],
            recv_sem=grad_sems.at[1, chunk],
            device_id={"tile": 1 - tile},
            device_id_type=MESH,
        )

    corner_copy = pltpu.make_async_remote_copy(
        src_ref=corners.at[0],
        dst_ref=corners.at[1],
        send_sem=corner_sems.at[0],
        recv_sem=corner_sems.at[1],
        device_id={"tile": 1 - tile},
        device_id_type=MESH,
    )
    corners[0, 0:8, :] = jnp.full((8, side), top_row, jnp.int32)
    corners[0, 8:16, :] = jnp.full((8, side), left_column, jnp.int32)

    def make_masks(place, first_row, first_column, keep):
        local_row = lax.broadcasted_iota(jnp.int32, (step, side), 0)
        local_column = lax.broadcasted_iota(jnp.int32, (step, side), 1)
        mine = jnp.where(local_column >= first_column, keep, 1.0 - keep)
        for chunk in range(chunks):
            for block in range(blocks):
                upper = jnp.where(local_row + (block * rows + chunk * step) >= first_row, mine, 0.0)
                masks[place, 0, chunk, block] = upper.astype(BF16)
                masks[place, 1, chunk, block] = (mine - upper).astype(BF16)

    keep = (1 - tile).astype(F32)

    @pl.when(is_top)
    def _():
        load_table.wait()
        for part in range(2):
            product = dot(row_move, table[part]).astype(BF16)
            for chunk in range(chunks):
                for c in range(2):
                    shifted[chunk, 2 * part + c] = product[
                        chunk * height : (chunk + 1) * height, c * side : (c + 1) * side
                    ]
        load_residual.wait()
        load_layers.wait()
        handed = conj_times(
            layers[0, 0, 0].astype(F32), layers[0, 0, 1].astype(F32), residual[0, 0], residual[0, 1]
        )
        handed = jnp.concatenate([handed[0].astype(BF16), handed[1].astype(BF16)], axis=1)
        for chunk in range(chunks):
            product = dot(shifted[chunk].reshape(4 * height, side), handed)
            by_real = product[:height] + product[2 * height : 3 * height]
            by_imag = product[height : 2 * height] + product[3 * height :]
            hand_out[chunk, 0] = (by_real[:, :side] - by_imag[:, side:]).astype(BF16)
            hand_out[chunk, 1] = (by_real[:, side:] + by_imag[:, :side]).astype(BF16)
            if chunk == 0:

                @pl.when(tile == 0)
                def _():
                    pl.semaphore_wait(barrier, 3)
                    pl.semaphore_signal(ready_sems.at[0], inc=1, device_id={"tile": 1}, device_id_type=MESH)

                @pl.when(tile == 1)
                def _():
                    pl.semaphore_wait(ready_sems.at[0], 1)

            hand_copy(chunk).start()
        corner_copy.start()
        load_waves.wait()
        gradient = conj_times(
            waves[0, 0, 0].astype(F32), waves[0, 0, 1].astype(F32), residual[0, 0], residual[0, 1]
        )
        moved = [roll(gradient[c].astype(BF16)).astype(BF16) for c in range(2)]
        for chunk in range(chunks):
            for c in range(2):
                grads[0, chunk, c] = moved[c][chunk * height : (chunk + 1) * height].reshape(blocks, step, side)
            grad_copy(chunk).start()
        make_masks(0, top_row, left_column, keep)

        @pl.when(tile == 1)
        def _():
            pl.semaphore_wait(barrier, 2 * probe_count - 1)
            pl.semaphore_signal(ready_sems.at[1], inc=1, device_id={"tile": 0}, device_id_type=MESH)

        @pl.when(tile == 0)
        def _():
            pl.semaphore_wait(ready_sems.at[1], 1)

    @pl.when(jnp.logical_not(is_top))
    def _():
        load_table.wait()
        row_back = onehot(column == (row + left_column) & (side - 1))
        for part in range(2):
            product = dot(row_back, table[part]).astype(BF16)
            for c in range(2):
                shifted[2 * part + c] = product[:, c * side : (c + 1) * side].reshape(chunks, height, side)
        load_waves.wait()
        for c in range(2):
            rolled[c] = roll(waves[0, 0, c]).astype(BF16)
        make_masks(0, top_row, left_column, keep)
        pl.semaphore_wait(barrier, probe_count)
        corner_copy.start()

    corner_copy.wait_recv()
    make_masks(1, corners[1, 0:1, :], corners[1, 8:9, :], keep)

    def strip(owner, chunk, c, kind):
        block, half = owner % blocks, owner // blocks
        return (
            grads[0, chunk, c, block].astype(kind) * masks[0, half, chunk, block].astype(kind)
            + grads[1, chunk, c, block].astype(kind) * masks[1, half, chunk, block].astype(kind)
        )

    def probe_copy(source, target, sems, chunk, low, high, mask):
        return pltpu.make_async_remote_copy(
            src_ref=source.at[chunk, low:high],
            dst_ref=target.at[chunk, low:high],
            send_sem=sems.at[0, chunk],
            recv_sem=sems.at[1, chunk],
            device_id={"probe": flip(probe, mask, probe_count)},
            device_id_type=MESH,
        )

    def far_copy(chunk):
        return probe_copy(far_out, far_in, far_sems, chunk, 0, pair_from[chunk], 3)

    def pair_copy(chunk):
        return probe_copy(far_out, pair_in, pair_sems, chunk, pair_from[chunk], 2, 1)

    def mid_copy(chunk):
        return probe_copy(mid_out, mid_in, mid_sems, chunk, 0, pair_from[chunk], 2)

    def sum_copy(chunk):
        return probe_copy(mid_out, mid_in, sum_sems, chunk, pair_from[chunk], 2, 2)

    def near_copy(chunk):
        return probe_copy(near_out, near_in, near_sems, chunk, 0, 2, 1)

    def copies(chunk):
        kinds = [near_copy]
        if pair_from[chunk] > 0:
            kinds += [far_copy, mid_copy]
        if pair_from[chunk] < 2:
            kinds += [pair_copy, sum_copy]
        return kinds

    def send_sums(chunk):
        if pair_from[chunk] < 2:
            pair_copy(chunk).wait_recv()
            for c in range(pair_from[chunk], 2):
                value = strip(flip(probe, 2, probe_count), chunk, c, F32) + pair_in[chunk, c].astype(F32)
                mid_out[chunk, c] = value.astype(BF16)
            sum_copy(chunk).start()

    for chunk in range(chunks):

        @pl.when(jnp.logical_not(is_top))
        def _():
            hand_copy(chunk).wait_recv()
            arrived = hand_in[chunk].reshape(2 * height, side)

            def times(c):
                high = shifted[c].reshape(side, side)
                low = shifted[2 + c].reshape(side, side)
                return dot(arrived, high) + dot(arrived, low)

            by_real, by_imag = times(0), times(1)
            real = by_real[:height] - by_imag[height:]
            imag = by_imag[:height] + by_real[height:]
            window = pl.ds(chunk * height, height)
            gradient = conj_times(rolled[0, window].astype(F32), rolled[1, window].astype(F32), real, imag)
            for c in range(2):
                grads[0, chunk, c] = gradient[c].astype(BF16).reshape(blocks, step, side)
            grad_copy(chunk).start()

        grad_copy(chunk).wait_recv()
        far = flip(probe, 3, probe_count)
        for c in range(1, -1, -1):
            far_out[chunk, c] = strip(far, chunk, c, BF16)
            if c == pair_from[chunk]:
                pair_copy(chunk).start()
        if pair_from[chunk] > 0:
            far_copy(chunk).start()
            for c in range(pair_from[chunk]):
                mid_out[chunk, c] = strip(flip(probe, 2, probe_count), chunk, c, BF16)
            mid_copy(chunk).start()
        for c in range(2):
            near_out[chunk, c] = strip(flip(probe, 1, probe_count), chunk, c, BF16)
        near_copy(chunk).start()
        window = pl.ds(chunk * step, step)
        for c in range(2):
            out[c, 0, window, :] = strip(probe, chunk, c, F32)
        if chunk >= lag:
            send_sums(chunk - lag)
    for chunk in range(max(chunks - lag, 0), chunks):
        send_sums(chunk)
    for chunk in range(chunks):
        window = pl.ds(chunk * step, step)
        near_copy(chunk).wait_recv()
        if pair_from[chunk] > 0:
            far_copy(chunk).wait_recv()
            mid_copy(chunk).wait_recv()
        if pair_from[chunk] < 2:
            sum_copy(chunk).wait_recv()
        for c in range(2):
            total = out[c, 0, window, :] + near_in[chunk, c].astype(F32) + mid_in[chunk, c].astype(F32)
            if c < pair_from[chunk]:
                total = total + far_in[chunk, c].astype(F32)
            out[c, 0, window, :] = total

    corner_copy.wait_send()
    for chunk in range(chunks):
        grad_copy(chunk).wait_send()
        for kind in copies(chunk):
            kind(chunk).wait_send()

    @pl.when(is_top)
    def _():
        for chunk in range(chunks):
            hand_copy(chunk).wait_send()


def rolled_call(waves, layers, residual, offsets, slot, rows, columns, chunks, pair_from, lag):
    side = waves.shape[-1]
    table = propagator(side)
    step = rows // chunks
    blocks = side // rows
    height = blocks * step
    hbm = pl.BlockSpec(memory_space=pltpu.HBM)
    strips = pltpu.VMEM((chunks, 2, step, columns), BF16)
    pairs = pltpu.SemaphoreType.DMA((2, chunks))
    return pl.pallas_call(
        functools.partial(rolled_kernel, chunks, pair_from, lag),
        out_shape=jax.ShapeDtypeStruct((2, 1, rows, columns), F32),
        in_specs=[hbm] * 4 + [pl.BlockSpec(memory_space=pltpu.SMEM), hbm],
        out_specs=pl.BlockSpec(memory_space=pltpu.VMEM),
        scratch_shapes=[
            pltpu.VMEM(waves.shape, waves.dtype),
            pltpu.VMEM(layers.shape, layers.dtype),
            pltpu.VMEM(residual.shape, residual.dtype),
            pltpu.VMEM(table.shape, BF16),
            pltpu.SMEM(offsets.shape[::-1], jnp.int32),
            pltpu.VMEM((4, 4, side // 4, side), BF16),
            pltpu.VMEM((chunks, 2, height, side), BF16),
            pltpu.VMEM((chunks, 2, height, side), BF16),
            pltpu.VMEM((2, side, side), BF16),
            pltpu.VMEM((2, chunks, 2, blocks, step, side), BF16),
            pltpu.VMEM((2, 2, chunks, blocks, step, side), BF16),
            pltpu.VMEM((2, 16, side), jnp.int32),
        ]
        + [strips] * 7
        + [pltpu.SemaphoreType.DMA((5,)), pairs, pairs, pltpu.SemaphoreType.DMA((2,))]
        + [pairs] * 5
        + [pltpu.SemaphoreType.REGULAR((2,))],
        compiler_params=pltpu.CompilerParams(
            collective_id=0, has_side_effects=True, vmem_limit_bytes=32 * 1024 * 1024
        ),
    )(
        *(
            pltpu.with_memory_space_constraint(x, pltpu.HBM)
            for x in (waves, layers, residual)
        ),
        pltpu.with_memory_space_constraint(offsets.T, pltpu.HBM),
        slot,
        pltpu.with_memory_space_constraint(jnp.asarray(table), pltpu.HBM),
    )


def per_device(depth_count, probe_count, tile_count, waves, layers, residual, offsets, slot):
    side = waves.shape[-1]
    rows, columns = OBJ // probe_count, OBJ // tile_count
    if (depth_count, probe_count, tile_count) == (2, 4, 2) and OBJ == 2 * side:
        return rolled_call(waves, layers, residual, offsets, slot, rows, columns, 4, (1, 1, 1, 1), 2)
    table = propagator(side)
    others = probe_count // 2 - 1
    vmem = pl.BlockSpec(memory_space=pltpu.VMEM)
    smem = pl.BlockSpec(memory_space=pltpu.SMEM)
    hbm = pl.BlockSpec(memory_space=pltpu.HBM)
    return pl.pallas_call(
        functools.partial(kernel, depth_count, probe_count),
        out_shape=jax.ShapeDtypeStruct((2, 1, rows, columns), F32),
        in_specs=[hbm, hbm, hbm, smem, smem, hbm],
        out_specs=vmem,
        scratch_shapes=[
            pltpu.VMEM(waves.shape, waves.dtype),
            pltpu.VMEM(layers.shape, layers.dtype),
            pltpu.VMEM(residual.shape, residual.dtype),
            pltpu.VMEM(table.shape, BF16),
            pltpu.VMEM((2, side, side), BF16),
            pltpu.VMEM((2, side, side), BF16),
            pltpu.VMEM((side, 2 * side), BF16),
            pltpu.VMEM((2, 2, side, side), BF16),
            pltpu.VMEM((2, 16, side), jnp.int32),
            pltpu.VMEM((probe_count, rows, columns), BF16),
            pltpu.VMEM((probe_count, rows, columns), BF16),
            pltpu.VMEM((others, rows, columns), BF16),
            pltpu.VMEM((others, rows, columns), BF16),
            pltpu.VMEM((others, rows, columns), BF16),
            pltpu.VMEM((others, rows, columns), BF16),
            pltpu.VMEM((others, rows, columns), F32),
            pltpu.SemaphoreType.DMA((4,)),
            pltpu.SemaphoreType.DMA((2, CHUNKS)),
            pltpu.SemaphoreType.DMA((2, CHUNKS)),
            pltpu.SemaphoreType.DMA((2,)),
            pltpu.SemaphoreType.DMA((2, probe_count)),
            pltpu.SemaphoreType.DMA((2, others)),
            pltpu.SemaphoreType.DMA((2, others)),
        ],
        compiler_params=pltpu.CompilerParams(
            collective_id=0, has_side_effects=True, vmem_limit_bytes=32 * 1024 * 1024
        ),
    )(
        *(pltpu.with_memory_space_constraint(x, pltpu.HBM) for x in (waves, layers, residual)),
        offsets.T,
        slot,
        pltpu.with_memory_space_constraint(jnp.asarray(table), pltpu.HBM),
    )


def solution(mesh):
    return jax.shard_map(
        functools.partial(per_device, mesh.shape["depth"], mesh.shape["probe"], mesh.shape["tile"]),
        mesh=mesh,
        in_specs=(
            P("depth", ("groups", "probe", "tile"), None, None, None),
            P("depth", ("groups", "probe", "tile"), None, None, None),
            P(("groups", "probe", "tile"), None, None, None),
            P("groups", None),
            P(("groups", "probe", "tile")),
        ),
        out_specs=P("groups", "depth", "probe", "tile"),
        check_vma=False,
    )
```

```python
import functools

import jax
import jax.numpy as jnp
import ml_dtypes
import numpy as np
from jax import lax
from jax.experimental import pallas as pl
from jax.experimental.pallas import tpu as pltpu
from jax.sharding import PartitionSpec as P

OBJ = 512
CHUNKS = 1
MESH = pl.DeviceIdType.MESH
F32 = jnp.float32
BF16 = jnp.bfloat16
KEPT = (6, 7)
TOP_MODES = ('d', 'd', 'd', 'r', 'r', 'r', 'r', 'r', 'r', 'r')
BOTTOM_MODES = ('r', 'r', 'd', 'd', 'r', 'r')
TOP_STEPS = ['g3', 'g0', 'g1', 'g2', 'g8', 'g9', 'g4', 'g5', 'g6', 'g7', 'm0', 'm1', 'd0', 'd1', 'd2', 'm2', 'm3', 'p3', 'p8', 's3', 'p9', 's8', 's9', 'p4', 'p5', 's4', 'p6', 's5', 'p7', 's6', 's7', 'a0', 'a1', 'a2', 'a3', 'a4', 'a5', 'a6', 'a7']
BOTTOM_STEPS = ['m0', 'm1', 'g0', 'm2', 'm3', 'g1', 'g2', 'g3', 'd2', 'g4', 'd3', 'g5', 'p0', 'p1', 's0', 's1', 'p4', 'p5', 's4', 's5', 'a0', 'a1', 'a2', 'a3', 'a4', 'a5', 'a8', 'a9']


def propagator(side):
    counter = np.arange(side)
    frequency = (counter + side // 2) % side - side // 2
    chirp = np.exp(0.5j * frequency.astype(np.float64) ** 2 / side)
    column = np.fft.ifft(chirp)
    matrix = column[(counter[:, None] - counter[None, :]) % side]
    parts = np.concatenate([matrix.real, matrix.imag], axis=1)
    high = parts.astype(ml_dtypes.bfloat16)
    low = (parts - high.astype(np.float64)).astype(ml_dtypes.bfloat16)
    return np.stack([high, low])


def dot(a, b):
    return jnp.dot(a, b, preferred_element_type=F32)


def split(value):
    high = value.astype(BF16)
    return high, (value - high.astype(F32)).astype(BF16)


def conj_times(layer_real, layer_imag, real, imag):
    return (
        layer_real * real + layer_imag * imag,
        layer_real * imag - layer_imag * real,
    )


def flip(index, mask, count):
    result, bit = 0, 1
    while bit < count:
        result = result + ((index // bit + (mask // bit) % 2) % 2) * bit
        bit *= 2
    return result


def kernel(
    depth_count,
    probe_count,
    waves_hbm,
    layers_hbm,
    residual_hbm,
    offsets,
    slot,
    table_hbm,
    out,
    waves,
    layers,
    residual,
    table,
    hand_out,
    hand_in,
    turned,
    grads,
    corners,
    direct_out,
    direct_in,
    pair_out,
    pair_in,
    sum_out,
    sum_in,
    held,
    load_sems,
    hand_sems,
    grad_sems,
    corner_sems,
    direct_sems,
    pair_sems,
    sum_sems,
):
    side = waves.shape[-1]
    rows, columns = out.shape[2], out.shape[3]
    step = side // CHUNKS
    depth = lax.axis_index("depth")
    probe = lax.axis_index("probe")
    tile = lax.axis_index("tile")
    is_top = depth == depth_count - 1
    has_below = depth > 0

    barrier = pltpu.get_barrier_semaphore()
    for mask in range(1, probe_count):
        pl.semaphore_signal(
            barrier, inc=1, device_id={"probe": flip(probe, mask, probe_count)}, device_id_type=MESH
        )
    pl.semaphore_signal(barrier, inc=1, device_id={"tile": 1 - tile}, device_id_type=MESH)

    @pl.when(depth < depth_count - 1)
    def _():
        pl.semaphore_signal(barrier, inc=1, device_id={"depth": depth + 1}, device_id_type=MESH)

    load_residual = pltpu.make_async_copy(residual_hbm, residual, load_sems.at[0])
    load_layers = pltpu.make_async_copy(layers_hbm, layers, load_sems.at[1])
    load_waves = pltpu.make_async_copy(waves_hbm, waves, load_sems.at[2])
    load_table = pltpu.make_async_copy(table_hbm, table, load_sems.at[3])

    @pl.when(is_top)
    def _():
        load_residual.start()

    if depth_count > 1:

        @pl.when(has_below)
        def _():
            load_layers.start()

        @pl.when(jnp.logical_not(is_top))
        def _():
            load_table.start()

    load_waves.start()

    own_slot = slot[0]
    top_row = offsets[0, own_slot]
    left_column = offsets[1, own_slot]
    corners[0, 0:8, :] = jnp.full((8, side), top_row, jnp.int32)
    corners[0, 8:16, :] = jnp.full((8, side), left_column, jnp.int32)

    @pl.when(has_below)
    def _():
        pl.semaphore_wait(barrier, probe_count + 1)

    @pl.when(jnp.logical_not(has_below))
    def _():
        pl.semaphore_wait(barrier, probe_count)

    corner_copy = pltpu.make_async_remote_copy(
        src_ref=corners.at[0],
        dst_ref=corners.at[1],
        send_sem=corner_sems.at[0],
        recv_sem=corner_sems.at[1],
        device_id={"tile": 1 - tile},
        device_id_type=MESH,
    )
    corner_copy.start()

    def hand_copy(part):
        window = pl.ds(part * step, step)
        return pltpu.make_async_remote_copy(
            src_ref=hand_out.at[:, window, :],
            dst_ref=hand_in.at[:, window, :],
            send_sem=hand_sems.at[0, part],
            recv_sem=hand_sems.at[1, part],
            device_id={"depth": depth - 1},
            device_id_type=MESH,
        )

    def grad_copy(part):
        window = pl.ds(part * step, step)
        return pltpu.make_async_remote_copy(
            src_ref=grads.at[0, :, window, :],
            dst_ref=grads.at[1, :, window, :],
            send_sem=grad_sems.at[0, part],
            recv_sem=grad_sems.at[1, part],
            device_id={"tile": 1 - tile},
            device_id_type=MESH,
        )

    def hand_down(part, real, imag):
        window = pl.ds(part * step, step)
        handed = conj_times(
            layers[0, 0, 0, window, :].astype(F32), layers[0, 0, 1, window, :].astype(F32), real, imag
        )
        hand_out[0, window, :] = handed[0].astype(BF16)
        hand_out[1, window, :] = handed[1].astype(BF16)
        hand_copy(part).start()

    def give_gradient(part, real, imag):
        window = pl.ds(part * step, step)
        gradient = conj_times(
            waves[0, 0, 0, window, :].astype(F32), waves[0, 0, 1, window, :].astype(F32), real, imag
        )
        grads[0, 0, window, :] = gradient[0].astype(BF16)
        grads[0, 1, window, :] = gradient[1].astype(BF16)
        grad_copy(part).start()

    @pl.when(is_top)
    def _():
        load_residual.wait()
        if depth_count > 1:
            load_layers.wait()
            for part in range(CHUNKS):
                window = pl.ds(part * step, step)
                hand_down(part, residual[0, 0, window, :], residual[0, 1, window, :])
        load_waves.wait()
        for part in range(CHUNKS):
            window = pl.ds(part * step, step)
            give_gradient(part, residual[0, 0, window, :], residual[0, 1, window, :])

    if depth_count > 1:

        @pl.when(jnp.logical_not(is_top))
        def _():
            load_table.wait()
            load_waves.wait()
            if depth_count > 2:

                @pl.when(has_below)
                def _():
                    load_layers.wait()

            for part in range(CHUNKS):
                window = pl.ds(part * step, step)
                hand_copy(part).wait_recv()
                real = dot(hand_in[0, window, :], table[0]) + dot(hand_in[0, window, :], table[1])
                imag = dot(hand_in[1, window, :], table[0]) + dot(hand_in[1, window, :], table[1])
                product = real[:, :side] - imag[:, side:], real[:, side:] + imag[:, :side]
                for c in range(2):
                    turned[window, pl.ds(c * side, side)] = product[c].astype(BF16)

            for part in range(CHUNKS):
                window = pl.ds(part * step, step)

                def from_left(index):
                    columns = pl.ds(index * side, side)
                    return (
                        dot(table[0, window, columns], turned[...]) + dot(table[1, window, columns], turned[...])
                    )

                by_real, by_imag = from_left(0), from_left(1)
                real = by_real[:, :side] - by_imag[:, side:]
                imag = by_real[:, side:] + by_imag[:, :side]
                if depth_count > 2:

                    @pl.when(has_below)
                    def _():
                        hand_down(part, real, imag)

                give_gradient(part, real, imag)

    row_index = lax.broadcasted_iota(jnp.int32, (side, columns), 0)
    column_index = lax.broadcasted_iota(jnp.int32, (side, columns), 1) + tile * columns

    def onehot(match):
        return jnp.where(match, 1.0, 0.0).astype(BF16)

    own_columns = onehot(column_index - row_index == left_column)
    placed = [[dot(grads[0, c], own_columns).astype(BF16)] for c in range(2)]

    corner_copy.wait_recv()
    for part in range(CHUNKS):
        grad_copy(part).wait_recv()
    peer_row = corners[1, 0:1, :]
    peer_columns = onehot(column_index - row_index == corners[1, 8:9, 0:columns])
    for c in range(2):
        placed[c].append(dot(grads[1, c], peer_columns).astype(BF16))

    strip_row = lax.broadcasted_iota(jnp.int32, (rows, side), 0)
    patch_row = lax.broadcasted_iota(jnp.int32, (rows, side), 1)
    distance = strip_row - patch_row

    def strip_part(owner, c):
        shifted = distance + owner * rows
        own_rows = onehot(shifted == top_row)
        peer_rows = onehot(shifted == peer_row)
        return dot(own_rows, placed[c][0]) + dot(peer_rows, placed[c][1])

    def strip(owner):
        return [strip_part(owner, c) for c in range(2)]

    def direct_copy(mask, c):
        place = mask - 1 if c == 0 else probe_count - 1
        return pltpu.make_async_remote_copy(
            src_ref=direct_out.at[place],
            dst_ref=direct_in.at[place],
            send_sem=direct_sems.at[0, place],
            recv_sem=direct_sems.at[1, place],
            device_id={"probe": flip(probe, mask, probe_count)},
            device_id_type=MESH,
        )

    def pair_copy(place):
        return pltpu.make_async_remote_copy(
            src_ref=pair_out.at[place],
            dst_ref=pair_in.at[place],
            send_sem=pair_sems.at[0, place],
            recv_sem=pair_sems.at[1, place],
            device_id={"probe": flip(probe, 1, probe_count)},
            device_id_type=MESH,
        )

    def sum_copy(place):
        return pltpu.make_async_remote_copy(
            src_ref=sum_out.at[place],
            dst_ref=sum_in.at[place],
            send_sem=sum_sems.at[0, place],
            recv_sem=sum_sems.at[1, place],
            device_id={"probe": flip(probe, 2 * place + 2, probe_count)},
            device_id_type=MESH,
        )

    others = range(probe_count // 2 - 1, 0, -1)
    for other in others:
        mask = 2 * other + 1
        owner = flip(probe, mask, probe_count)
        pair_out[other - 1] = strip_part(owner, 1).astype(BF16)
        pair_copy(other - 1).start()
        direct_out[mask - 1] = strip_part(owner, 0).astype(BF16)
        direct_copy(mask, 0).start()
    for other in others:
        mask = 2 * other
        real, imag = strip(flip(probe, mask, probe_count))
        direct_out[mask - 1] = real.astype(BF16)
        direct_copy(mask, 0).start()
        held[other - 1] = imag
    real, imag = strip(flip(probe, 1, probe_count))
    direct_out[0] = real.astype(BF16)
    direct_out[probe_count - 1] = imag.astype(BF16)
    direct_copy(1, 0).start()
    direct_copy(1, 1).start()
    for other in others:
        pair_copy(other - 1).wait_recv()
        sum_out[other - 1] = (held[other - 1] + pair_in[other - 1].astype(F32)).astype(BF16)
        sum_copy(other - 1).start()
    total = strip(probe)
    for c in range(2):
        out[c, 0] = total[c]
    for mask in range(probe_count - 1, 0, -1):
        direct_copy(mask, 0).wait_recv()
        out[0, 0] += direct_in[mask - 1].astype(F32)
    direct_copy(1, 1).wait_recv()
    out[1, 0] += direct_in[probe_count - 1].astype(F32)
    for other in others:
        sum_copy(other - 1).wait_recv()
        out[1, 0] += sum_in[other - 1].astype(F32)

    corner_copy.wait_send()
    for part in range(CHUNKS):
        grad_copy(part).wait_send()
    for mask in range(1, probe_count):
        direct_copy(mask, 0).wait_send()
    direct_copy(1, 1).wait_send()
    for other in others:
        pair_copy(other - 1).wait_send()
        sum_copy(other - 1).wait_send()

    @pl.when(has_below)
    def _():
        for part in range(CHUNKS):
            hand_copy(part).wait_send()


def rolled_kernel(
    kept,
    top_modes,
    bottom_modes,
    top_order,
    bottom_order,
    waves_hbm,
    layers_hbm,
    residual_hbm,
    offsets_hbm,
    slot,
    table_hbm,
    out,
    waves,
    layers,
    residual,
    table,
    offsets,
    left_table,
    right_table,
    hand_out,
    hand_in,
    rolled,
    rolled_in,
    grads,
    grads_in,
    near_in,
    far_in,
    near_out,
    far_out,
    masks,
    near_masks,
    corners,
    mid_out,
    mid_in,
    own_out,
    own_in,
    load_sems,
    hand_sems,
    rolled_sems,
    corner_sems,
    tile_sems,
    near_sems,
    pass_sems,
    mid_sems,
    far_sems,
    wide_sems,
    own_sems,
    ready_sems,
):
    side = waves.shape[-1]
    rows = out.shape[2]
    step = rolled.shape[2]
    units = side // step
    chunks = rows // step
    depth = lax.axis_index("depth")
    probe = lax.axis_index("probe")
    tile = lax.axis_index("tile")
    is_top = depth == 1
    is_bottom = depth == 0
    block = probe % 2
    half = probe // 2

    def at_probe(mask):
        return flip(probe, mask, 4)

    barrier = pltpu.get_barrier_semaphore()

    def greet(device):
        pl.semaphore_signal(barrier, inc=1, device_id=device, device_id_type=MESH)

    greet({"depth": 1 - depth, "tile": 0})
    greet({"tile": 1 - tile})
    for mask in range(1, 4):
        greet({"probe": at_probe(mask), "tile": 1})

    @pl.when(is_bottom)
    def _():
        for mask in range(1, 4):
            greet({"probe": at_probe(mask), "depth": 1, "tile": 1})

    def wait_depth():
        @pl.when(tile == 0)
        def _():
            pl.semaphore_wait(barrier, 3)
            pl.semaphore_signal(ready_sems.at[0], inc=1, device_id={"tile": 1}, device_id_type=MESH)

        @pl.when(tile == 1)
        def _():
            pl.semaphore_wait(ready_sems.at[0], 1)

    def wait_probe(count):
        @pl.when(tile == 1)
        def _():
            pl.semaphore_wait(barrier, count)
            pl.semaphore_signal(ready_sems.at[1], inc=1, device_id={"tile": 0}, device_id_type=MESH)

        @pl.when(tile == 0)
        def _():
            pl.semaphore_wait(ready_sems.at[1], 1)

    load_offsets = pltpu.make_async_copy(offsets_hbm, offsets, load_sems.at[4])
    load_residual = pltpu.make_async_copy(residual_hbm, residual, load_sems.at[0])
    load_layers = pltpu.make_async_copy(layers_hbm, layers, load_sems.at[1])
    load_waves = pltpu.make_async_copy(waves_hbm, waves, load_sems.at[2])
    load_table = pltpu.make_async_copy(table_hbm, table, load_sems.at[3])
    load_offsets.start()

    @pl.when(is_top)
    def _():
        load_table.start()
        load_residual.start()
        load_layers.start()
        load_waves.start()

    @pl.when(is_bottom)
    def _():
        load_waves.start()
        load_table.start()

    load_offsets.wait()
    own_slot = slot[0]
    top_row = offsets[0, own_slot]
    left_column = offsets[1, own_slot]

    def onehot(match):
        return jnp.where(match, 1.0, 0.0).astype(BF16)

    row = lax.broadcasted_iota(jnp.int32, (side, side), 0)
    column = lax.broadcasted_iota(jnp.int32, (side, side), 1)
    row_move = onehot(column == ((row - top_row) & (side - 1)))
    column_move = onehot(row == ((column - left_column) & (side - 1)))

    def roll(value):
        return dot(dot(row_move, value).astype(BF16), column_move).astype(BF16)

    def roll_right_table():
        row_back = onehot(column == ((row + left_column) & (side - 1)))
        for part in range(2):
            right_table[part] = dot(row_back, table[part]).astype(BF16)

    def remote(source, target, sems, index, device):
        return pltpu.make_async_remote_copy(
            src_ref=source,
            dst_ref=target,
            send_sem=sems.at[0, index],
            recv_sem=sems.at[1, index],
            device_id=device,
            device_id_type=MESH,
        )

    def hand_copy(unit):
        return remote(hand_out.at[unit], hand_in.at[unit], hand_sems, unit, {"depth": 0})

    def corner_copy(place):
        device = [None, {"tile": 1 - tile}, {"probe": at_probe(1)}, {"probe": at_probe(1), "tile": 1 - tile}]
        return remote(corners.at[0], corners.at[place], corner_sems, place, device[place])

    def tile_copy(job):
        return remote(grads.at[job], grads_in.at[job], tile_sems, job, {"tile": 1 - tile})

    def rolled_copy(place):
        return remote(rolled.at[kept[place]], rolled_in.at[place], rolled_sems, place, {"depth": 1})

    def leave(job, mask):
        device = {"probe": at_probe(mask)} if mask else {}
        if job >= units:
            device["depth"] = 0
        return device

    def near_copy(job, direct):
        if direct:
            return remote(near_out.at[job], near_in.at[0, job], near_sems, job, leave(job, 1))
        return remote(grads.at[job], near_in.at[0, job], near_sems, job, {"probe": at_probe(1)})

    def wide_copy(job):
        device = {"probe": at_probe(1), "tile": 1 - tile}
        return remote(grads.at[job], near_in.at[1, job], wide_sems, job, device)

    def far_copy(job):
        return remote(far_out.at[job], far_in.at[job], far_sems, job, leave(job, 3))

    def pass_copy(job):
        return remote(near_in.at[0, job], near_in.at[1, job], pass_sems, job, {"tile": 1 - tile})

    def mid_copy(job):
        return remote(mid_out.at[job], mid_in.at[job], mid_sems, job, leave(job, 2))

    def own_copy(job):
        return remote(own_out.at[job - units], own_in.at[job - units], own_sems, job - units, leave(job, 0))

    def fill_corners():
        corners[0, 0:8, :] = jnp.full((8, side), top_row, jnp.int32)
        corners[0, 8:16, :] = jnp.full((8, side), left_column, jnp.int32)

    def make_masks(target, place, count, first):
        local_row = lax.broadcasted_iota(jnp.int32, (step, side), 0) + first
        local_column = lax.broadcasted_iota(jnp.int32, (step, side), 1)
        keep = (1 - tile).astype(F32)
        mine = jnp.where(local_column >= corners[place, 8:9, :], keep, 1.0 - keep)
        for unit in range(count):
            upper = jnp.where(local_row + unit * step >= corners[place, 0:1, :], mine, 0.0)
            target[place % 2, 0, unit] = upper.astype(BF16)
            target[place % 2, 1, unit] = (mine - upper).astype(BF16)

    def right_product(arrived):
        product = dot(arrived, right_table[0]) + dot(arrived, right_table[1])
        real = product[:step, :side] - product[step:, side:]
        imag = product[:step, side:] + product[step:, :side]
        return real, imag

    def put_gradient(job, gradient):
        for c in range(2):
            grads[job, c] = gradient[c].astype(BF16)

    def unit_of(job):
        return job if job < units else kept[job - units]

    def window_of(job):
        return pl.ds(unit_of(job) % chunks * step, step)

    def keeps(job):
        return block == unit_of(job) // chunks

    def gives(job):
        return block != unit_of(job) // chunks

    def strip(job, which, c, near):
        sources = [(grads, masks.at[0]), (grads_in, masks.at[1])]
        total = None
        for value, mask in sources:
            term = value[job, c].astype(F32) * mask[which, unit_of(job)].astype(F32)
            total = term if total is None else total + term
        for place in range(2 if near else 0):
            mask = near_masks[place, which, unit_of(job) % chunks].astype(F32)
            total = total + near_in[place, job, c].astype(F32) * mask
        return total

    def keep_strips(job, near):
        for c in range(2):
            mid_out[job, c] = strip(job, 1 - half, c, near).astype(BF16)
        mid_copy(job).start()
        for c in range(2):
            value = strip(job, half, c, near)
            if job < units:
                out[c, 0, window_of(job), :] = value
            else:
                own_out[job - units, c] = value.astype(BF16)
        if job >= units:
            own_copy(job).start()

    def stage_sum(job):
        @pl.when(keeps(job))
        def _():
            tile_copy(job).wait_recv()
            pass_copy(job).wait_recv()
            keep_strips(job, True)

    def stage_wide(job):
        @pl.when(keeps(job))
        def _():
            tile_copy(job).wait_recv()
            near_copy(job, False).wait_recv()
            wide_copy(job).wait_recv()
            keep_strips(job, True)

    def stage_direct(job):
        tile_copy(job).wait_recv()

        @pl.when(gives(job))
        def _():
            for c in range(2):
                far_out[job, c] = strip(job, 1 - half, c, False).astype(BF16)
            far_copy(job).start()
            for c in range(2):
                near_out[job, c] = strip(job, half, c, False).astype(BF16)
            near_copy(job, True).start()

        @pl.when(keeps(job))
        def _():
            keep_strips(job, False)

    def stage_pass(job):
        @pl.when(keeps(job))
        def _():
            near_copy(job, False).wait_recv()
            pass_copy(job).start()

    def stage_add(job, direct):
        @pl.when(keeps(job))
        def _():
            if job < units:
                first = [out[c, 0, window_of(job), :] for c in range(2)]
            else:
                own_copy(job).wait_recv()
                first = [own_in[job - units, c].astype(F32) for c in range(2)]
            if direct:
                near_copy(job, True).wait_recv()
                far_copy(job).wait_recv()
            mid_copy(job).wait_recv()
            for c in range(2):
                total = first[c] + mid_in[job, c].astype(F32)
                if direct:
                    total = total + near_in[0, job, c].astype(F32) + far_in[job, c].astype(F32)
                out[c, 0, window_of(job), :] = total

    def stage_masks(place):
        if place > 0:
            corner_copy(place).wait_recv()
        if place < 2:
            make_masks(masks, place, units, 0)
        else:
            make_masks(near_masks, place, chunks, block * rows)

    def send(job, mode):
        if mode == "d":
            tile_copy(job).start()
        else:

            @pl.when(keeps(job))
            def _():
                tile_copy(job).start()

            @pl.when(gives(job))
            def _():
                near_copy(job, False).start()
                if mode == "w":
                    wide_copy(job).start()

    def finish(job, mode):
        if mode == "d":
            tile_copy(job).wait_send()

        @pl.when(keeps(job))
        def _():
            if mode != "d":
                tile_copy(job).wait_send()
            if mode == "r":
                pass_copy(job).wait_send()
            mid_copy(job).wait_send()
            if job >= units:
                own_copy(job).wait_send()

        @pl.when(gives(job))
        def _():
            near_copy(job, mode == "d").wait_send()
            if mode == "d":
                far_copy(job).wait_send()
            if mode == "w":
                wide_copy(job).wait_send()

    def run(order, modes, jobs, stage_gradient):
        stages = dict(
            g=stage_gradient,
            m=stage_masks,
            d=stage_direct,
            p=stage_pass,
            s=stage_sum,
            w=stage_wide,
            a=lambda job: stage_add(job, (top_modes if job >= units else modes)[job] == "d"),
        )
        for kind, number in order:
            stages[kind](number)
        for place in range(1, 4):
            corner_copy(place).wait_send()
        for job in jobs:
            finish(job, modes[job])

    @pl.when(is_top)
    def _():
        fill_corners()
        load_table.wait()
        for part in range(2):
            product = dot(row_move, table[part]).astype(BF16)
            for unit in range(units):
                for c in range(2):
                    left_table[unit, 2 * part + c] = product[
                        unit * step : (unit + 1) * step, c * side : (c + 1) * side
                    ]
        load_residual.wait()
        load_layers.wait()
        handed = conj_times(
            layers[0, 0, 0].astype(F32), layers[0, 0, 1].astype(F32), residual[0, 0], residual[0, 1]
        )
        handed = jnp.concatenate([handed[0].astype(BF16), handed[1].astype(BF16)], axis=1)
        first = True
        for unit in [number for kind, number in bottom_order if kind == "g"] + list(kept):
            product = dot(left_table[unit].reshape(4 * step, side), handed)
            by_real = product[:step] + product[2 * step : 3 * step]
            by_imag = product[step : 2 * step] + product[3 * step :]
            hand_out[unit, 0] = (by_real[:, :side] - by_imag[:, side:]).astype(BF16)
            hand_out[unit, 1] = (by_real[:, side:] + by_imag[:, :side]).astype(BF16)
            if first:
                wait_depth()
                first = False
            if unit not in kept:
                hand_copy(unit).start()
        corner_copy(1).start()
        load_waves.wait()
        gradient = conj_times(
            waves[0, 0, 0].astype(F32), waves[0, 0, 1].astype(F32), residual[0, 0], residual[0, 1]
        )
        gradient = [roll(gradient[c].astype(BF16)) for c in range(2)]
        for unit in range(units):
            put_gradient(unit, [gradient[c][unit * step : (unit + 1) * step] for c in range(2)])
        wait_probe(13)
        corner_copy(2).start()
        corner_copy(3).start()

        def stage_gradient(job):
            if job == units:
                roll_right_table()
            if job >= units:
                real, imag = right_product(hand_out[unit_of(job)].reshape(2 * step, side))
                rolled_copy(job - units).wait_recv()
                source = rolled_in[job - units].astype(F32)
                put_gradient(job, conj_times(source[0], source[1], real, imag))
            send(job, top_modes[job])

        run(top_order, top_modes, range(units + len(kept)), stage_gradient)
        for unit in range(units):
            if unit not in kept:
                hand_copy(unit).wait_send()

    @pl.when(is_bottom)
    def _():
        fill_corners()
        load_waves.wait()
        source = [roll(waves[0, 0, c]) for c in range(2)]
        for unit in range(units):
            for c in range(2):
                rolled[unit, c] = source[c][unit * step : (unit + 1) * step]
        wait_depth()
        for place in range(len(kept)):
            rolled_copy(place).start()
        corner_copy(1).start()
        load_table.wait()
        roll_right_table()
        wait_probe(7)
        corner_copy(2).start()
        corner_copy(3).start()

        def stage_gradient(job):
            hand_copy(job).wait_recv()
            real, imag = right_product(hand_in[job].reshape(2 * step, side))
            source = rolled[job].astype(F32)
            put_gradient(job, conj_times(source[0], source[1], real, imag))
            send(job, bottom_modes[job])

        jobs = [unit for unit in range(units) if unit not in kept]
        run(bottom_order, bottom_modes, jobs, stage_gradient)
        for place in range(len(kept)):
            rolled_copy(place).wait_send()


def orders(text):
    return [(step[0], int(step[1:])) for step in text]


def rolled_call(waves, layers, residual, offsets, slot, rows, columns, step, kept, top, bottom):
    side = waves.shape[-1]
    table = propagator(side)
    units = side // step
    jobs = units + len(kept)
    hbm = pl.BlockSpec(memory_space=pltpu.HBM)

    def copies(count):
        return pltpu.SemaphoreType.DMA((2, count))

    return pl.pallas_call(
        functools.partial(rolled_kernel, kept, top, bottom, orders(TOP_STEPS), orders(BOTTOM_STEPS)),
        out_shape=jax.ShapeDtypeStruct((2, 1, rows, columns), F32),
        in_specs=[hbm] * 4 + [pl.BlockSpec(memory_space=pltpu.SMEM), hbm],
        out_specs=pl.BlockSpec(memory_space=pltpu.VMEM),
        scratch_shapes=[
            pltpu.VMEM(waves.shape, waves.dtype),
            pltpu.VMEM(layers.shape, layers.dtype),
            pltpu.VMEM(residual.shape, residual.dtype),
            pltpu.VMEM(table.shape, BF16),
            pltpu.SMEM(offsets.shape[::-1], jnp.int32),
            pltpu.VMEM((units, 4, step, side), BF16),
            pltpu.VMEM(table.shape, BF16),
            pltpu.VMEM((units, 2, step, side), BF16),
            pltpu.VMEM((units, 2, step, side), BF16),
            pltpu.VMEM((units, 2, step, side), BF16),
            pltpu.VMEM((max(len(kept), 1), 2, step, side), BF16),
            pltpu.VMEM((jobs, 2, step, side), BF16),
            pltpu.VMEM((jobs, 2, step, side), BF16),
            pltpu.VMEM((2, jobs, 2, step, side), BF16),
            pltpu.VMEM((jobs, 2, step, side), BF16),
            pltpu.VMEM((jobs, 2, step, side), BF16),
            pltpu.VMEM((jobs, 2, step, side), BF16),
            pltpu.VMEM((2, 2, units, step, side), BF16),
            pltpu.VMEM((2, 2, rows // step, step, side), BF16),
            pltpu.VMEM((4, 16, side), jnp.int32),
            pltpu.VMEM((jobs, 2, step, columns), BF16),
            pltpu.VMEM((jobs, 2, step, columns), BF16),
            pltpu.VMEM((max(len(kept), 1), 2, step, columns), BF16),
            pltpu.VMEM((max(len(kept), 1), 2, step, columns), BF16),
            pltpu.SemaphoreType.DMA((5,)),
            copies(units),
            copies(max(len(kept), 1)),
            copies(4),
            copies(jobs),
            copies(jobs),
            copies(jobs),
            copies(jobs),
            copies(jobs),
            copies(jobs),
            copies(max(len(kept), 1)),
            pltpu.SemaphoreType.REGULAR((2,)),
        ],
        compiler_params=pltpu.CompilerParams(
            collective_id=0, has_side_effects=True, vmem_limit_bytes=32 * 1024 * 1024
        ),
    )(
        *(pltpu.with_memory_space_constraint(x, pltpu.HBM) for x in (waves, layers, residual, offsets.T)),
        slot,
        pltpu.with_memory_space_constraint(jnp.asarray(table), pltpu.HBM),
    )


def per_device(depth_count, probe_count, tile_count, waves, layers, residual, offsets, slot):
    side = waves.shape[-1]
    rows, columns = OBJ // probe_count, OBJ // tile_count
    if (depth_count, probe_count, tile_count) == (2, 4, 2) and OBJ == 2 * side:
        return rolled_call(
            waves, layers, residual, offsets, slot, rows, columns, 32, KEPT, TOP_MODES, BOTTOM_MODES
        )
    table = propagator(side)
    others = probe_count // 2 - 1
    vmem = pl.BlockSpec(memory_space=pltpu.VMEM)
    smem = pl.BlockSpec(memory_space=pltpu.SMEM)
    hbm = pl.BlockSpec(memory_space=pltpu.HBM)
    return pl.pallas_call(
        functools.partial(kernel, depth_count, probe_count),
        out_shape=jax.ShapeDtypeStruct((2, 1, rows, columns), F32),
        in_specs=[hbm, hbm, hbm, smem, smem, hbm],
        out_specs=vmem,
        scratch_shapes=[
            pltpu.VMEM(waves.shape, waves.dtype),
            pltpu.VMEM(layers.shape, layers.dtype),
            pltpu.VMEM(residual.shape, residual.dtype),
            pltpu.VMEM(table.shape, BF16),
            pltpu.VMEM((2, side, side), BF16),
            pltpu.VMEM((2, side, side), BF16),
            pltpu.VMEM((side, 2 * side), BF16),
            pltpu.VMEM((2, 2, side, side), BF16),
            pltpu.VMEM((2, 16, side), jnp.int32),
            pltpu.VMEM((probe_count, rows, columns), BF16),
            pltpu.VMEM((probe_count, rows, columns), BF16),
            pltpu.VMEM((others, rows, columns), BF16),
            pltpu.VMEM((others, rows, columns), BF16),
            pltpu.VMEM((others, rows, columns), BF16),
            pltpu.VMEM((others, rows, columns), BF16),
            pltpu.VMEM((others, rows, columns), F32),
            pltpu.SemaphoreType.DMA((4,)),
            pltpu.SemaphoreType.DMA((2, CHUNKS)),
            pltpu.SemaphoreType.DMA((2, CHUNKS)),
            pltpu.SemaphoreType.DMA((2,)),
            pltpu.SemaphoreType.DMA((2, probe_count)),
            pltpu.SemaphoreType.DMA((2, others)),
            pltpu.SemaphoreType.DMA((2, others)),
        ],
        compiler_params=pltpu.CompilerParams(
            collective_id=0, has_side_effects=True, vmem_limit_bytes=32 * 1024 * 1024
        ),
    )(
        *(pltpu.with_memory_space_constraint(x, pltpu.HBM) for x in (waves, layers, residual)),
        offsets.T,
        slot,
        pltpu.with_memory_space_constraint(jnp.asarray(table), pltpu.HBM),
    )


def solution(mesh):
    return jax.shard_map(
        functools.partial(per_device, mesh.shape["depth"], mesh.shape["probe"], mesh.shape["tile"]),
        mesh=mesh,
        in_specs=(
            P("depth", ("groups", "probe", "tile"), None, None, None),
            P("depth", ("groups", "probe", "tile"), None, None, None),
            P(("groups", "probe", "tile"), None, None, None),
            P("groups", None),
            P(("groups", "probe", "tile")),
        ),
        out_specs=P("groups", "depth", "probe", "tile"),
        check_vma=False,
    )
```

```python
import functools

import jax
import jax.numpy as jnp
import ml_dtypes
import numpy as np
from jax import lax
from jax.experimental import pallas as pl
from jax.experimental.pallas import tpu as pltpu
from jax.sharding import PartitionSpec as P

OBJ = 512
CHUNKS = 1
MESH = pl.DeviceIdType.MESH
F32 = jnp.float32
BF16 = jnp.bfloat16
KEPT = (7,)
TOP_MODES = ('d', 'd', 'd', 'r', 'r', 'r', 'r', 'r', 'w')
BOTTOM_MODES = ('r', 'r', 'd', 'd', 'r', 'r', 'w', 'r')
TOP_STEPS = ['g3', 'g0', 'g1', 'g2', 'g4', 'g5', 'g6', 'g7', 'g8', 'm0', 'm1', 'd0', 'd1', 'd2', 'p3', 'p4', 'p5', 'm2', 'm3', 's3', 's4', 'p6', 'w8', 's5', 'p7', 's6', 's7', 'a0', 'a1', 'a2', 'a3', 'a4', 'a5', 'a6', 'a7']
BOTTOM_STEPS = ['m0', 'm1', 'g0', 'g1', 'g2', 'g3', 'd2', 'g4', 'p0', 'd3', 'g5', 'p1', 'm2', 'm3', 's0', 'g6', 's1', 'p4', 'p5', 's4', 's5', 'w6', 'a2', 'a8', 'a3', 'a0', 'a1', 'a4', 'a5', 'a6']


def propagator(side):
    counter = np.arange(side)
    frequency = (counter + side // 2) % side - side // 2
    chirp = np.exp(0.5j * frequency.astype(np.float64) ** 2 / side)
    column = np.fft.ifft(chirp)
    matrix = column[(counter[:, None] - counter[None, :]) % side]
    parts = np.concatenate([matrix.real, matrix.imag], axis=1)
    high = parts.astype(ml_dtypes.bfloat16)
    low = (parts - high.astype(np.float64)).astype(ml_dtypes.bfloat16)
    return np.stack([high, low])


def dot(a, b):
    return jnp.dot(a, b, preferred_element_type=F32)


def split(value):
    high = value.astype(BF16)
    return high, (value - high.astype(F32)).astype(BF16)


def conj_times(layer_real, layer_imag, real, imag):
    return (
        layer_real * real + layer_imag * imag,
        layer_real * imag - layer_imag * real,
    )


def flip(index, mask, count):
    result, bit = 0, 1
    while bit < count:
        result = result + ((index // bit + (mask // bit) % 2) % 2) * bit
        bit *= 2
    return result


def kernel(
    depth_count,
    probe_count,
    waves_hbm,
    layers_hbm,
    residual_hbm,
    offsets,
    slot,
    table_hbm,
    out,
    waves,
    layers,
    residual,
    table,
    hand_out,
    hand_in,
    turned,
    grads,
    corners,
    direct_out,
    direct_in,
    pair_out,
    pair_in,
    sum_out,
    sum_in,
    held,
    load_sems,
    hand_sems,
    grad_sems,
    corner_sems,
    direct_sems,
    pair_sems,
    sum_sems,
):
    side = waves.shape[-1]
    rows, columns = out.shape[2], out.shape[3]
    step = side // CHUNKS
    depth = lax.axis_index("depth")
    probe = lax.axis_index("probe")
    tile = lax.axis_index("tile")
    is_top = depth == depth_count - 1
    has_below = depth > 0

    barrier = pltpu.get_barrier_semaphore()
    for mask in range(1, probe_count):
        pl.semaphore_signal(
            barrier, inc=1, device_id={"probe": flip(probe, mask, probe_count)}, device_id_type=MESH
        )
    pl.semaphore_signal(barrier, inc=1, device_id={"tile": 1 - tile}, device_id_type=MESH)

    @pl.when(depth < depth_count - 1)
    def _():
        pl.semaphore_signal(barrier, inc=1, device_id={"depth": depth + 1}, device_id_type=MESH)

    load_residual = pltpu.make_async_copy(residual_hbm, residual, load_sems.at[0])
    load_layers = pltpu.make_async_copy(layers_hbm, layers, load_sems.at[1])
    load_waves = pltpu.make_async_copy(waves_hbm, waves, load_sems.at[2])
    load_table = pltpu.make_async_copy(table_hbm, table, load_sems.at[3])

    @pl.when(is_top)
    def _():
        load_residual.start()

    if depth_count > 1:

        @pl.when(has_below)
        def _():
            load_layers.start()

        @pl.when(jnp.logical_not(is_top))
        def _():
            load_table.start()

    load_waves.start()

    own_slot = slot[0]
    top_row = offsets[0, own_slot]
    left_column = offsets[1, own_slot]
    corners[0, 0:8, :] = jnp.full((8, side), top_row, jnp.int32)
    corners[0, 8:16, :] = jnp.full((8, side), left_column, jnp.int32)

    @pl.when(has_below)
    def _():
        pl.semaphore_wait(barrier, probe_count + 1)

    @pl.when(jnp.logical_not(has_below))
    def _():
        pl.semaphore_wait(barrier, probe_count)

    corner_copy = pltpu.make_async_remote_copy(
        src_ref=corners.at[0],
        dst_ref=corners.at[1],
        send_sem=corner_sems.at[0],
        recv_sem=corner_sems.at[1],
        device_id={"tile": 1 - tile},
        device_id_type=MESH,
    )
    corner_copy.start()

    def hand_copy(part):
        window = pl.ds(part * step, step)
        return pltpu.make_async_remote_copy(
            src_ref=hand_out.at[:, window, :],
            dst_ref=hand_in.at[:, window, :],
            send_sem=hand_sems.at[0, part],
            recv_sem=hand_sems.at[1, part],
            device_id={"depth": depth - 1},
            device_id_type=MESH,
        )

    def grad_copy(part):
        window = pl.ds(part * step, step)
        return pltpu.make_async_remote_copy(
            src_ref=grads.at[0, :, window, :],
            dst_ref=grads.at[1, :, window, :],
            send_sem=grad_sems.at[0, part],
            recv_sem=grad_sems.at[1, part],
            device_id={"tile": 1 - tile},
            device_id_type=MESH,
        )

    def hand_down(part, real, imag):
        window = pl.ds(part * step, step)
        handed = conj_times(
            layers[0, 0, 0, window, :].astype(F32), layers[0, 0, 1, window, :].astype(F32), real, imag
        )
        hand_out[0, window, :] = handed[0].astype(BF16)
        hand_out[1, window, :] = handed[1].astype(BF16)
        hand_copy(part).start()

    def give_gradient(part, real, imag):
        window = pl.ds(part * step, step)
        gradient = conj_times(
            waves[0, 0, 0, window, :].astype(F32), waves[0, 0, 1, window, :].astype(F32), real, imag
        )
        grads[0, 0, window, :] = gradient[0].astype(BF16)
        grads[0, 1, window, :] = gradient[1].astype(BF16)
        grad_copy(part).start()

    @pl.when(is_top)
    def _():
        load_residual.wait()
        if depth_count > 1:
            load_layers.wait()
            for part in range(CHUNKS):
                window = pl.ds(part * step, step)
                hand_down(part, residual[0, 0, window, :], residual[0, 1, window, :])
        load_waves.wait()
        for part in range(CHUNKS):
            window = pl.ds(part * step, step)
            give_gradient(part, residual[0, 0, window, :], residual[0, 1, window, :])

    if depth_count > 1:

        @pl.when(jnp.logical_not(is_top))
        def _():
            load_table.wait()
            load_waves.wait()
            if depth_count > 2:

                @pl.when(has_below)
                def _():
                    load_layers.wait()

            for part in range(CHUNKS):
                window = pl.ds(part * step, step)
                hand_copy(part).wait_recv()
                real = dot(hand_in[0, window, :], table[0]) + dot(hand_in[0, window, :], table[1])
                imag = dot(hand_in[1, window, :], table[0]) + dot(hand_in[1, window, :], table[1])
                product = real[:, :side] - imag[:, side:], real[:, side:] + imag[:, :side]
                for c in range(2):
                    turned[window, pl.ds(c * side, side)] = product[c].astype(BF16)

            for part in range(CHUNKS):
                window = pl.ds(part * step, step)

                def from_left(index):
                    columns = pl.ds(index * side, side)
                    return (
                        dot(table[0, window, columns], turned[...]) + dot(table[1, window, columns], turned[...])
                    )

                by_real, by_imag = from_left(0), from_left(1)
                real = by_real[:, :side] - by_imag[:, side:]
                imag = by_real[:, side:] + by_imag[:, :side]
                if depth_count > 2:

                    @pl.when(has_below)
                    def _():
                        hand_down(part, real, imag)

                give_gradient(part, real, imag)

    row_index = lax.broadcasted_iota(jnp.int32, (side, columns), 0)
    column_index = lax.broadcasted_iota(jnp.int32, (side, columns), 1) + tile * columns

    def onehot(match):
        return jnp.where(match, 1.0, 0.0).astype(BF16)

    own_columns = onehot(column_index - row_index == left_column)
    placed = [[dot(grads[0, c], own_columns).astype(BF16)] for c in range(2)]

    corner_copy.wait_recv()
    for part in range(CHUNKS):
        grad_copy(part).wait_recv()
    peer_row = corners[1, 0:1, :]
    peer_columns = onehot(column_index - row_index == corners[1, 8:9, 0:columns])
    for c in range(2):
        placed[c].append(dot(grads[1, c], peer_columns).astype(BF16))

    strip_row = lax.broadcasted_iota(jnp.int32, (rows, side), 0)
    patch_row = lax.broadcasted_iota(jnp.int32, (rows, side), 1)
    distance = strip_row - patch_row

    def strip_part(owner, c):
        shifted = distance + owner * rows
        own_rows = onehot(shifted == top_row)
        peer_rows = onehot(shifted == peer_row)
        return dot(own_rows, placed[c][0]) + dot(peer_rows, placed[c][1])

    def strip(owner):
        return [strip_part(owner, c) for c in range(2)]

    def direct_copy(mask, c):
        place = mask - 1 if c == 0 else probe_count - 1
        return pltpu.make_async_remote_copy(
            src_ref=direct_out.at[place],
            dst_ref=direct_in.at[place],
            send_sem=direct_sems.at[0, place],
            recv_sem=direct_sems.at[1, place],
            device_id={"probe": flip(probe, mask, probe_count)},
            device_id_type=MESH,
        )

    def pair_copy(place):
        return pltpu.make_async_remote_copy(
            src_ref=pair_out.at[place],
            dst_ref=pair_in.at[place],
            send_sem=pair_sems.at[0, place],
            recv_sem=pair_sems.at[1, place],
            device_id={"probe": flip(probe, 1, probe_count)},
            device_id_type=MESH,
        )

    def sum_copy(place):
        return pltpu.make_async_remote_copy(
            src_ref=sum_out.at[place],
            dst_ref=sum_in.at[place],
            send_sem=sum_sems.at[0, place],
            recv_sem=sum_sems.at[1, place],
            device_id={"probe": flip(probe, 2 * place + 2, probe_count)},
            device_id_type=MESH,
        )

    others = range(probe_count // 2 - 1, 0, -1)
    for other in others:
        mask = 2 * other + 1
        owner = flip(probe, mask, probe_count)
        pair_out[other - 1] = strip_part(owner, 1).astype(BF16)
        pair_copy(other - 1).start()
        direct_out[mask - 1] = strip_part(owner, 0).astype(BF16)
        direct_copy(mask, 0).start()
    for other in others:
        mask = 2 * other
        real, imag = strip(flip(probe, mask, probe_count))
        direct_out[mask - 1] = real.astype(BF16)
        direct_copy(mask, 0).start()
        held[other - 1] = imag
    real, imag = strip(flip(probe, 1, probe_count))
    direct_out[0] = real.astype(BF16)
    direct_out[probe_count - 1] = imag.astype(BF16)
    direct_copy(1, 0).start()
    direct_copy(1, 1).start()
    for other in others:
        pair_copy(other - 1).wait_recv()
        sum_out[other - 1] = (held[other - 1] + pair_in[other - 1].astype(F32)).astype(BF16)
        sum_copy(other - 1).start()
    total = strip(probe)
    for c in range(2):
        out[c, 0] = total[c]
    for mask in range(probe_count - 1, 0, -1):
        direct_copy(mask, 0).wait_recv()
        out[0, 0] += direct_in[mask - 1].astype(F32)
    direct_copy(1, 1).wait_recv()
    out[1, 0] += direct_in[probe_count - 1].astype(F32)
    for other in others:
        sum_copy(other - 1).wait_recv()
        out[1, 0] += sum_in[other - 1].astype(F32)

    corner_copy.wait_send()
    for part in range(CHUNKS):
        grad_copy(part).wait_send()
    for mask in range(1, probe_count):
        direct_copy(mask, 0).wait_send()
    direct_copy(1, 1).wait_send()
    for other in others:
        pair_copy(other - 1).wait_send()
        sum_copy(other - 1).wait_send()

    @pl.when(has_below)
    def _():
        for part in range(CHUNKS):
            hand_copy(part).wait_send()


def rolled_kernel(
    kept,
    top_modes,
    bottom_modes,
    top_order,
    bottom_order,
    waves_hbm,
    layers_hbm,
    residual_hbm,
    offsets_hbm,
    slot,
    table_hbm,
    out,
    waves,
    layers,
    residual,
    table,
    offsets,
    left_table,
    right_table,
    hand_out,
    hand_in,
    rolled,
    rolled_in,
    grads,
    grads_in,
    near_in,
    far_in,
    near_out,
    far_out,
    masks,
    near_masks,
    corners,
    mid_out,
    mid_in,
    own_out,
    own_in,
    load_sems,
    send_sems,
    hand_sems,
    rolled_sems,
    corner_sems,
    tile_sems,
    near_sems,
    aux_sems,
    mid_sems,
    own_sems,
    ready_sems,
):
    side = waves.shape[-1]
    rows = out.shape[2]
    step = rolled.shape[2]
    units = side // step
    chunks = rows // step
    depth = lax.axis_index("depth")
    probe = lax.axis_index("probe")
    tile = lax.axis_index("tile")
    is_top = depth == 1
    is_bottom = depth == 0
    block = probe % 2
    half = probe // 2

    def at_probe(mask):
        return flip(probe, mask, 4)

    barrier = pltpu.get_barrier_semaphore()

    def greet(device):
        pl.semaphore_signal(barrier, inc=1, device_id=device, device_id_type=MESH)

    greet({"depth": 1 - depth, "tile": 0})
    greet({"tile": 1 - tile})
    for mask in range(1, 4):
        greet({"probe": at_probe(mask), "tile": 1})

    @pl.when(is_bottom)
    def _():
        for mask in range(1, 4):
            greet({"probe": at_probe(mask), "depth": 1, "tile": 1})

    def wait_depth():
        @pl.when(tile == 0)
        def _():
            pl.semaphore_wait(barrier, 3)
            pl.semaphore_signal(ready_sems.at[0], inc=1, device_id={"tile": 1}, device_id_type=MESH)

        @pl.when(tile == 1)
        def _():
            pl.semaphore_wait(ready_sems.at[0], 1)

    def wait_probe(count):
        @pl.when(tile == 1)
        def _():
            pl.semaphore_wait(barrier, count)
            pl.semaphore_signal(ready_sems.at[1], inc=1, device_id={"tile": 0}, device_id_type=MESH)

        @pl.when(tile == 0)
        def _():
            pl.semaphore_wait(ready_sems.at[1], 1)

    load_offsets = pltpu.make_async_copy(offsets_hbm, offsets, load_sems.at[4])
    load_residual = pltpu.make_async_copy(residual_hbm, residual, load_sems.at[0])
    load_layers = pltpu.make_async_copy(layers_hbm, layers, load_sems.at[1])
    load_waves = pltpu.make_async_copy(waves_hbm, waves, load_sems.at[2])
    load_table = pltpu.make_async_copy(table_hbm, table, load_sems.at[3])
    load_offsets.start()

    @pl.when(is_top)
    def _():
        load_table.start()
        load_residual.start()
        load_layers.start()
        load_waves.start()

    @pl.when(is_bottom)
    def _():
        load_waves.start()
        load_table.start()

    load_offsets.wait()
    own_slot = slot[0]
    top_row = offsets[0, own_slot]
    left_column = offsets[1, own_slot]

    def onehot(match):
        return jnp.where(match, 1.0, 0.0).astype(BF16)

    row = lax.broadcasted_iota(jnp.int32, (side, side), 0)
    column = lax.broadcasted_iota(jnp.int32, (side, side), 1)
    row_move = onehot(column == ((row - top_row) & (side - 1)))
    column_move = onehot(row == ((column - left_column) & (side - 1)))

    def roll(value):
        return dot(dot(row_move, value).astype(BF16), column_move).astype(BF16)

    def roll_right_table():
        row_back = onehot(column == ((row + left_column) & (side - 1)))
        for part in range(2):
            right_table[part] = dot(row_back, table[part]).astype(BF16)

    kinds = ("hand", "rolled", "corner", "tile", "near", "aux", "mid", "own")

    def remote(kind, source, target, received, device):
        return pltpu.make_async_remote_copy(
            src_ref=source,
            dst_ref=target,
            send_sem=send_sems.at[kinds.index(kind)],
            recv_sem=received,
            device_id=device,
            device_id_type=MESH,
        )

    def unit_of(job):
        return job if job < units else kept[job - units]

    def place_of(job):
        return job % chunks if job < units else chunks + job - units

    def hand_copy(unit):
        return remote("hand", hand_out.at[unit], hand_in.at[unit], hand_sems.at[unit], {"depth": 0})

    def rolled_copy(place):
        source = rolled.at[kept[place]]
        return remote("rolled", source, rolled_in.at[place], rolled_sems.at[place], {"depth": 1})

    def corner_copy(place):
        device = [None, {"tile": 1 - tile}, {"probe": at_probe(1)}, {"probe": at_probe(1), "tile": 1 - tile}]
        return remote("corner", corners.at[0], corners.at[place], corner_sems.at[place - 1], device[place])

    def tile_copy(job):
        return remote("tile", grads.at[job], grads_in.at[job], tile_sems.at[job], {"tile": 1 - tile})

    def leave(job, mask):
        device = {"probe": at_probe(mask)} if mask else {}
        if job >= units:
            device["depth"] = 0
        return device

    def near_copy(job, direct):
        source, device = (near_out, leave(job, 1)) if direct else (grads, {"probe": at_probe(1)})
        return remote("near", source.at[job], near_in.at[0, job], near_sems.at[place_of(job)], device)

    def wide_copy(job):
        device = {"probe": at_probe(1), "tile": 1 - tile}
        return remote("aux", grads.at[job], near_in.at[1, job], aux_sems.at[place_of(job)], device)

    def far_copy(job):
        return remote("aux", far_out.at[job], far_in.at[job], aux_sems.at[place_of(job)], leave(job, 3))

    def pass_copy(job):
        source = near_in.at[0, job]
        return remote("aux", source, near_in.at[1, job], aux_sems.at[place_of(job)], {"tile": 1 - tile})

    def mid_copy(job):
        return remote("mid", mid_out.at[job], mid_in.at[job], mid_sems.at[place_of(job)], leave(job, 2))

    def own_copy(job):
        place = job - units
        return remote("own", own_out.at[place], own_in.at[place], own_sems.at[place], leave(job, 0))

    def wait_sent(kind, source, count):
        if count:
            remote(kind, source.at[0:count], source.at[0:count], corner_sems.at[0], {"tile": 1 - tile}).wait_send()

    def fill_corners():
        corners[0, 0:8, :] = jnp.full((8, side), top_row, jnp.int32)
        corners[0, 8:16, :] = jnp.full((8, side), left_column, jnp.int32)

    def make_masks(target, place, count, first):
        local_row = lax.broadcasted_iota(jnp.int32, (step, side), 0) + first
        local_column = lax.broadcasted_iota(jnp.int32, (step, side), 1)
        keep = (1 - tile).astype(F32)
        mine = jnp.where(local_column >= corners[place, 8:9, :], keep, 1.0 - keep)
        for unit in range(count):
            upper = jnp.where(local_row + unit * step >= corners[place, 0:1, :], mine, 0.0)
            target[place % 2, 0, unit] = upper.astype(BF16)
            target[place % 2, 1, unit] = (mine - upper).astype(BF16)

    def right_product(arrived):
        product = dot(arrived, right_table[0]) + dot(arrived, right_table[1])
        real = product[:step, :side] - product[step:, side:]
        imag = product[:step, side:] + product[step:, :side]
        return real, imag

    def put_gradient(job, gradient):
        for c in range(2):
            grads[job, c] = gradient[c].astype(BF16)

    def window_of(job):
        return pl.ds(unit_of(job) % chunks * step, step)

    def keeps(job):
        return block == unit_of(job) // chunks

    def gives(job):
        return block != unit_of(job) // chunks

    def strip(job, which, c, near):
        sources = [(grads, masks.at[0]), (grads_in, masks.at[1])]
        total = None
        for value, mask in sources:
            term = value[job, c].astype(F32) * mask[which, unit_of(job)].astype(F32)
            total = term if total is None else total + term
        for place in range(2 if near else 0):
            mask = near_masks[place, which, unit_of(job) % chunks].astype(F32)
            total = total + near_in[place, job, c].astype(F32) * mask
        return total

    def keep_strips(job, near):
        for c in range(2):
            mid_out[job, c] = strip(job, 1 - half, c, near).astype(BF16)
        mid_copy(job).start()
        for c in range(2):
            value = strip(job, half, c, near)
            if job < units:
                out[c, 0, window_of(job), :] = value
            else:
                own_out[job - units, c] = value.astype(BF16)
        if job >= units:
            own_copy(job).start()

    def stage_sum(job):
        @pl.when(keeps(job))
        def _():
            tile_copy(job).wait_recv()
            pass_copy(job).wait_recv()
            keep_strips(job, True)

    def stage_wide(job):
        @pl.when(keeps(job))
        def _():
            tile_copy(job).wait_recv()
            near_copy(job, False).wait_recv()
            wide_copy(job).wait_recv()
            keep_strips(job, True)

    def stage_direct(job):
        tile_copy(job).wait_recv()

        @pl.when(gives(job))
        def _():
            for c in range(2):
                far_out[job, c] = strip(job, 1 - half, c, False).astype(BF16)
            far_copy(job).start()
            for c in range(2):
                near_out[job, c] = strip(job, half, c, False).astype(BF16)
            near_copy(job, True).start()

        @pl.when(keeps(job))
        def _():
            keep_strips(job, False)

    def stage_pass(job):
        @pl.when(keeps(job))
        def _():
            near_copy(job, False).wait_recv()
            pass_copy(job).start()

    def stage_add(job, direct):
        @pl.when(keeps(job))
        def _():
            if job < units:
                first = [out[c, 0, window_of(job), :] for c in range(2)]
            else:
                own_copy(job).wait_recv()
                first = [own_in[job - units, c].astype(F32) for c in range(2)]
            if direct:
                near_copy(job, True).wait_recv()
                far_copy(job).wait_recv()
            mid_copy(job).wait_recv()
            for c in range(2):
                total = first[c] + mid_in[job, c].astype(F32)
                if direct:
                    total = total + near_in[0, job, c].astype(F32) + far_in[job, c].astype(F32)
                out[c, 0, window_of(job), :] = total

    def stage_masks(place):
        if place > 0:
            corner_copy(place).wait_recv()
        if place < 2:
            make_masks(masks, place, units, 0)
        else:
            make_masks(near_masks, place, chunks, block * rows)

    def send(job, mode):
        if mode == "d":
            tile_copy(job).start()
        else:

            @pl.when(keeps(job))
            def _():
                tile_copy(job).start()

            @pl.when(gives(job))
            def _():
                near_copy(job, False).start()
                if mode == "w":
                    wide_copy(job).start()

    def finish(jobs, modes):
        for half_units in range(2):
            count = dict.fromkeys(kinds, 0)
            for job in jobs:
                own_half = unit_of(job) // chunks == half_units
                mode = modes[job]
                count["tile"] += own_half or mode == "d"
                count["mid"] += own_half
                count["own"] += own_half and job >= units
                count["near"] += not own_half
                count["aux"] += mode == "r" if own_half else mode != "r"

            @pl.when(block == half_units)
            def _():
                wait_sent("tile", grads, count["tile"])
                wait_sent("near", grads, count["near"])
                wait_sent("aux", grads, count["aux"])
                wait_sent("mid", mid_out, count["mid"])
                wait_sent("own", own_out, count["own"])

    def run(order, modes, jobs, stage_gradient):
        stages = dict(
            g=stage_gradient,
            m=stage_masks,
            d=stage_direct,
            p=stage_pass,
            s=stage_sum,
            w=stage_wide,
            a=lambda job: stage_add(job, (top_modes if job >= units else modes)[job] == "d"),
        )
        for kind, number in order:
            stages[kind](number)
        wait_sent("corner", corners, 3)
        finish(jobs, modes)

    @pl.when(is_top)
    def _():
        fill_corners()
        load_table.wait()
        for part in range(2):
            product = dot(row_move, table[part]).astype(BF16)
            for unit in range(units):
                for c in range(2):
                    left_table[unit, 2 * part + c] = product[
                        unit * step : (unit + 1) * step, c * side : (c + 1) * side
                    ]
        load_residual.wait()
        load_layers.wait()
        handed = conj_times(
            layers[0, 0, 0].astype(F32), layers[0, 0, 1].astype(F32), residual[0, 0], residual[0, 1]
        )
        handed = jnp.concatenate([handed[0].astype(BF16), handed[1].astype(BF16)], axis=1)
        first = True
        for unit in [number for kind, number in bottom_order if kind == "g"] + list(kept):
            product = dot(left_table[unit].reshape(4 * step, side), handed)
            by_real = product[:step] + product[2 * step : 3 * step]
            by_imag = product[step : 2 * step] + product[3 * step :]
            hand_out[unit, 0] = (by_real[:, :side] - by_imag[:, side:]).astype(BF16)
            hand_out[unit, 1] = (by_real[:, side:] + by_imag[:, :side]).astype(BF16)
            if first:
                wait_depth()
                first = False
            if unit not in kept:
                hand_copy(unit).start()
        corner_copy(1).start()
        load_waves.wait()
        gradient = conj_times(
            waves[0, 0, 0].astype(F32), waves[0, 0, 1].astype(F32), residual[0, 0], residual[0, 1]
        )
        gradient = [roll(gradient[c].astype(BF16)) for c in range(2)]
        for unit in range(units):
            put_gradient(unit, [gradient[c][unit * step : (unit + 1) * step] for c in range(2)])
        wait_probe(13)
        corner_copy(2).start()
        corner_copy(3).start()

        def stage_gradient(job):
            if job == units:
                roll_right_table()
            if job >= units:
                real, imag = right_product(hand_out[unit_of(job)].reshape(2 * step, side))
                rolled_copy(job - units).wait_recv()
                source = rolled_in[job - units].astype(F32)
                put_gradient(job, conj_times(source[0], source[1], real, imag))
            send(job, top_modes[job])

        run(top_order, top_modes, range(units + len(kept)), stage_gradient)
        wait_sent("hand", hand_out, units - len(kept))

    @pl.when(is_bottom)
    def _():
        fill_corners()
        load_waves.wait()
        source = [roll(waves[0, 0, c]) for c in range(2)]
        for unit in range(units):
            for c in range(2):
                rolled[unit, c] = source[c][unit * step : (unit + 1) * step]
        wait_depth()
        for place in range(len(kept)):
            rolled_copy(place).start()
        corner_copy(1).start()
        load_table.wait()
        roll_right_table()
        wait_probe(7)
        corner_copy(2).start()
        corner_copy(3).start()

        def stage_gradient(job):
            hand_copy(job).wait_recv()
            real, imag = right_product(hand_in[job].reshape(2 * step, side))
            source = rolled[job].astype(F32)
            put_gradient(job, conj_times(source[0], source[1], real, imag))
            send(job, bottom_modes[job])

        jobs = [unit for unit in range(units) if unit not in kept]
        run(bottom_order, bottom_modes, jobs, stage_gradient)
        wait_sent("rolled", rolled, len(kept))


def orders(text):
    return [(step[0], int(step[1:])) for step in text]


def rolled_call(waves, layers, residual, offsets, slot, rows, columns, step, kept, top, bottom):
    side = waves.shape[-1]
    table = propagator(side)
    units = side // step
    jobs = units + len(kept)
    hbm = pl.BlockSpec(memory_space=pltpu.HBM)

    def copies(count):
        return pltpu.SemaphoreType.DMA((count,))

    return pl.pallas_call(
        functools.partial(rolled_kernel, kept, top, bottom, orders(TOP_STEPS), orders(BOTTOM_STEPS)),
        out_shape=jax.ShapeDtypeStruct((2, 1, rows, columns), F32),
        in_specs=[hbm] * 4 + [pl.BlockSpec(memory_space=pltpu.SMEM), hbm],
        out_specs=pl.BlockSpec(memory_space=pltpu.VMEM),
        scratch_shapes=[
            pltpu.VMEM(waves.shape, waves.dtype),
            pltpu.VMEM(layers.shape, layers.dtype),
            pltpu.VMEM(residual.shape, residual.dtype),
            pltpu.VMEM(table.shape, BF16),
            pltpu.SMEM(offsets.shape[::-1], jnp.int32),
            pltpu.VMEM((units, 4, step, side), BF16),
            pltpu.VMEM(table.shape, BF16),
            pltpu.VMEM((units, 2, step, side), BF16),
            pltpu.VMEM((units, 2, step, side), BF16),
            pltpu.VMEM((units, 2, step, side), BF16),
            pltpu.VMEM((max(len(kept), 1), 2, step, side), BF16),
            pltpu.VMEM((jobs, 2, step, side), BF16),
            pltpu.VMEM((jobs, 2, step, side), BF16),
            pltpu.VMEM((2, jobs, 2, step, side), BF16),
            pltpu.VMEM((jobs, 2, step, side), BF16),
            pltpu.VMEM((jobs, 2, step, side), BF16),
            pltpu.VMEM((jobs, 2, step, side), BF16),
            pltpu.VMEM((2, 2, units, step, side), BF16),
            pltpu.VMEM((2, 2, rows // step, step, side), BF16),
            pltpu.VMEM((4, 16, side), jnp.int32),
            pltpu.VMEM((jobs, 2, step, columns), BF16),
            pltpu.VMEM((jobs, 2, step, columns), BF16),
            pltpu.VMEM((max(len(kept), 1), 2, step, columns), BF16),
            pltpu.VMEM((max(len(kept), 1), 2, step, columns), BF16),
            pltpu.SemaphoreType.DMA((5,)),
            copies(8),
            copies(units),
            copies(max(len(kept), 1)),
            copies(3),
            copies(jobs),
            copies(rows // step + len(kept)),
            copies(rows // step + len(kept)),
            copies(rows // step + len(kept)),
            copies(max(len(kept), 1)),
            pltpu.SemaphoreType.REGULAR((2,)),
        ],
        compiler_params=pltpu.CompilerParams(
            collective_id=0, has_side_effects=True, vmem_limit_bytes=32 * 1024 * 1024
        ),
    )(
        *(pltpu.with_memory_space_constraint(x, pltpu.HBM) for x in (waves, layers, residual, offsets.T)),
        slot,
        pltpu.with_memory_space_constraint(jnp.asarray(table), pltpu.HBM),
    )


def per_device(depth_count, probe_count, tile_count, waves, layers, residual, offsets, slot):
    side = waves.shape[-1]
    rows, columns = OBJ // probe_count, OBJ // tile_count
    if (depth_count, probe_count, tile_count) == (2, 4, 2) and OBJ == 2 * side:
        return rolled_call(
            waves, layers, residual, offsets, slot, rows, columns, 32, KEPT, TOP_MODES, BOTTOM_MODES
        )
    table = propagator(side)
    others = probe_count // 2 - 1
    vmem = pl.BlockSpec(memory_space=pltpu.VMEM)
    smem = pl.BlockSpec(memory_space=pltpu.SMEM)
    hbm = pl.BlockSpec(memory_space=pltpu.HBM)
    return pl.pallas_call(
        functools.partial(kernel, depth_count, probe_count),
        out_shape=jax.ShapeDtypeStruct((2, 1, rows, columns), F32),
        in_specs=[hbm, hbm, hbm, smem, smem, hbm],
        out_specs=vmem,
        scratch_shapes=[
            pltpu.VMEM(waves.shape, waves.dtype),
            pltpu.VMEM(layers.shape, layers.dtype),
            pltpu.VMEM(residual.shape, residual.dtype),
            pltpu.VMEM(table.shape, BF16),
            pltpu.VMEM((2, side, side), BF16),
            pltpu.VMEM((2, side, side), BF16),
            pltpu.VMEM((side, 2 * side), BF16),
            pltpu.VMEM((2, 2, side, side), BF16),
            pltpu.VMEM((2, 16, side), jnp.int32),
            pltpu.VMEM((probe_count, rows, columns), BF16),
            pltpu.VMEM((probe_count, rows, columns), BF16),
            pltpu.VMEM((others, rows, columns), BF16),
            pltpu.VMEM((others, rows, columns), BF16),
            pltpu.VMEM((others, rows, columns), BF16),
            pltpu.VMEM((others, rows, columns), BF16),
            pltpu.VMEM((others, rows, columns), F32),
            pltpu.SemaphoreType.DMA((4,)),
            pltpu.SemaphoreType.DMA((2, CHUNKS)),
            pltpu.SemaphoreType.DMA((2, CHUNKS)),
            pltpu.SemaphoreType.DMA((2,)),
            pltpu.SemaphoreType.DMA((2, probe_count)),
            pltpu.SemaphoreType.DMA((2, others)),
            pltpu.SemaphoreType.DMA((2, others)),
        ],
        compiler_params=pltpu.CompilerParams(
            collective_id=0, has_side_effects=True, vmem_limit_bytes=32 * 1024 * 1024
        ),
    )(
        *(pltpu.with_memory_space_constraint(x, pltpu.HBM) for x in (waves, layers, residual)),
        offsets.T,
        slot,
        pltpu.with_memory_space_constraint(jnp.asarray(table), pltpu.HBM),
    )


def solution(mesh):
    return jax.shard_map(
        functools.partial(per_device, mesh.shape["depth"], mesh.shape["probe"], mesh.shape["tile"]),
        mesh=mesh,
        in_specs=(
            P("depth", ("groups", "probe", "tile"), None, None, None),
            P("depth", ("groups", "probe", "tile"), None, None, None),
            P(("groups", "probe", "tile"), None, None, None),
            P("groups", None),
            P(("groups", "probe", "tile")),
        ),
        out_specs=P("groups", "depth", "probe", "tile"),
        check_vma=False,
    )
```

```python
import functools

import jax
import jax.numpy as jnp
import ml_dtypes
import numpy as np
from jax import lax
from jax.experimental import pallas as pl
from jax.experimental.pallas import tpu as pltpu
from jax.sharding import PartitionSpec as P

OBJ = 512
CHUNKS = 1
MESH = pl.DeviceIdType.MESH
F32 = jnp.float32
BF16 = jnp.bfloat16
KEPT = (7,)
TOP_MODES = ('d', 'd', 'd', 'w', 'r', 'r', 'r', 'd', 'w')
BOTTOM_MODES = ('r', 'r', 'd', 'd', 'r', 'r', 'w', 'd')
TOP_STEPS = ['g3', 'g0', 'g1', 'g2', 'g4', 'g5', 'g6', 'g7', 'g8', 'm0', 'm1', 'd0', 'd1', 'd2', 'd7', 'p4', 'm2', 'm3', 'w3', 'p5', 's4', 'p6', 'w8', 's5', 's6', 'a0', 'a1', 'a2', 'a7', 'a3', 'a4', 'a5', 'a6']
BOTTOM_STEPS = ['m0', 'm1', 'g0', 'g2', 'g1', 'd2', 'g3', 'g4', 'p0', 'd3', 'g5', 'm2', 'm3', 's0', 'g6', 'p1', 's1', 'p4', 'p5', 's4', 's5', 'w6', 'a2', 'a8', 'a3', 'a0', 'a1', 'a4', 'a5', 'a6']


def propagator(side):
    counter = np.arange(side)
    frequency = (counter + side // 2) % side - side // 2
    chirp = np.exp(0.5j * frequency.astype(np.float64) ** 2 / side)
    column = np.fft.ifft(chirp)
    matrix = column[(counter[:, None] - counter[None, :]) % side]
    parts = np.concatenate([matrix.real, matrix.imag], axis=1)
    high = parts.astype(ml_dtypes.bfloat16)
    low = (parts - high.astype(np.float64)).astype(ml_dtypes.bfloat16)
    return np.stack([high, low])


def dot(a, b):
    return jnp.dot(a, b, preferred_element_type=F32)


def split(value):
    high = value.astype(BF16)
    return high, (value - high.astype(F32)).astype(BF16)


def conj_times(layer_real, layer_imag, real, imag):
    return (
        layer_real * real + layer_imag * imag,
        layer_real * imag - layer_imag * real,
    )


def flip(index, mask, count):
    result, bit = 0, 1
    while bit < count:
        result = result + ((index // bit + (mask // bit) % 2) % 2) * bit
        bit *= 2
    return result


def kernel(
    depth_count,
    probe_count,
    waves_hbm,
    layers_hbm,
    residual_hbm,
    offsets,
    slot,
    table_hbm,
    out,
    waves,
    layers,
    residual,
    table,
    hand_out,
    hand_in,
    turned,
    grads,
    corners,
    direct_out,
    direct_in,
    pair_out,
    pair_in,
    sum_out,
    sum_in,
    held,
    load_sems,
    hand_sems,
    grad_sems,
    corner_sems,
    direct_sems,
    pair_sems,
    sum_sems,
):
    side = waves.shape[-1]
    rows, columns = out.shape[2], out.shape[3]
    step = side // CHUNKS
    depth = lax.axis_index("depth")
    probe = lax.axis_index("probe")
    tile = lax.axis_index("tile")
    is_top = depth == depth_count - 1
    has_below = depth > 0

    barrier = pltpu.get_barrier_semaphore()
    for mask in range(1, probe_count):
        pl.semaphore_signal(
            barrier, inc=1, device_id={"probe": flip(probe, mask, probe_count)}, device_id_type=MESH
        )
    pl.semaphore_signal(barrier, inc=1, device_id={"tile": 1 - tile}, device_id_type=MESH)

    @pl.when(depth < depth_count - 1)
    def _():
        pl.semaphore_signal(barrier, inc=1, device_id={"depth": depth + 1}, device_id_type=MESH)

    load_residual = pltpu.make_async_copy(residual_hbm, residual, load_sems.at[0])
    load_layers = pltpu.make_async_copy(layers_hbm, layers, load_sems.at[1])
    load_waves = pltpu.make_async_copy(waves_hbm, waves, load_sems.at[2])
    load_table = pltpu.make_async_copy(table_hbm, table, load_sems.at[3])

    @pl.when(is_top)
    def _():
        load_residual.start()

    if depth_count > 1:

        @pl.when(has_below)
        def _():
            load_layers.start()

        @pl.when(jnp.logical_not(is_top))
        def _():
            load_table.start()

    load_waves.start()

    own_slot = slot[0]
    top_row = offsets[0, own_slot]
    left_column = offsets[1, own_slot]
    corners[0, 0:8, :] = jnp.full((8, side), top_row, jnp.int32)
    corners[0, 8:16, :] = jnp.full((8, side), left_column, jnp.int32)

    @pl.when(has_below)
    def _():
        pl.semaphore_wait(barrier, probe_count + 1)

    @pl.when(jnp.logical_not(has_below))
    def _():
        pl.semaphore_wait(barrier, probe_count)

    corner_copy = pltpu.make_async_remote_copy(
        src_ref=corners.at[0],
        dst_ref=corners.at[1],
        send_sem=corner_sems.at[0],
        recv_sem=corner_sems.at[1],
        device_id={"tile": 1 - tile},
        device_id_type=MESH,
    )
    corner_copy.start()

    def hand_copy(part):
        window = pl.ds(part * step, step)
        return pltpu.make_async_remote_copy(
            src_ref=hand_out.at[:, window, :],
            dst_ref=hand_in.at[:, window, :],
            send_sem=hand_sems.at[0, part],
            recv_sem=hand_sems.at[1, part],
            device_id={"depth": depth - 1},
            device_id_type=MESH,
        )

    def grad_copy(part):
        window = pl.ds(part * step, step)
        return pltpu.make_async_remote_copy(
            src_ref=grads.at[0, :, window, :],
            dst_ref=grads.at[1, :, window, :],
            send_sem=grad_sems.at[0, part],
            recv_sem=grad_sems.at[1, part],
            device_id={"tile": 1 - tile},
            device_id_type=MESH,
        )

    def hand_down(part, real, imag):
        window = pl.ds(part * step, step)
        handed = conj_times(
            layers[0, 0, 0, window, :].astype(F32), layers[0, 0, 1, window, :].astype(F32), real, imag
        )
        hand_out[0, window, :] = handed[0].astype(BF16)
        hand_out[1, window, :] = handed[1].astype(BF16)
        hand_copy(part).start()

    def give_gradient(part, real, imag):
        window = pl.ds(part * step, step)
        gradient = conj_times(
            waves[0, 0, 0, window, :].astype(F32), waves[0, 0, 1, window, :].astype(F32), real, imag
        )
        grads[0, 0, window, :] = gradient[0].astype(BF16)
        grads[0, 1, window, :] = gradient[1].astype(BF16)
        grad_copy(part).start()

    @pl.when(is_top)
    def _():
        load_residual.wait()
        if depth_count > 1:
            load_layers.wait()
            for part in range(CHUNKS):
                window = pl.ds(part * step, step)
                hand_down(part, residual[0, 0, window, :], residual[0, 1, window, :])
        load_waves.wait()
        for part in range(CHUNKS):
            window = pl.ds(part * step, step)
            give_gradient(part, residual[0, 0, window, :], residual[0, 1, window, :])

    if depth_count > 1:

        @pl.when(jnp.logical_not(is_top))
        def _():
            load_table.wait()
            load_waves.wait()
            if depth_count > 2:

                @pl.when(has_below)
                def _():
                    load_layers.wait()

            for part in range(CHUNKS):
                window = pl.ds(part * step, step)
                hand_copy(part).wait_recv()
                real = dot(hand_in[0, window, :], table[0]) + dot(hand_in[0, window, :], table[1])
                imag = dot(hand_in[1, window, :], table[0]) + dot(hand_in[1, window, :], table[1])
                product = real[:, :side] - imag[:, side:], real[:, side:] + imag[:, :side]
                for c in range(2):
                    turned[window, pl.ds(c * side, side)] = product[c].astype(BF16)

            for part in range(CHUNKS):
                window = pl.ds(part * step, step)

                def from_left(index):
                    columns = pl.ds(index * side, side)
                    return (
                        dot(table[0, window, columns], turned[...]) + dot(table[1, window, columns], turned[...])
                    )

                by_real, by_imag = from_left(0), from_left(1)
                real = by_real[:, :side] - by_imag[:, side:]
                imag = by_real[:, side:] + by_imag[:, :side]
                if depth_count > 2:

                    @pl.when(has_below)
                    def _():
                        hand_down(part, real, imag)

                give_gradient(part, real, imag)

    row_index = lax.broadcasted_iota(jnp.int32, (side, columns), 0)
    column_index = lax.broadcasted_iota(jnp.int32, (side, columns), 1) + tile * columns

    def onehot(match):
        return jnp.where(match, 1.0, 0.0).astype(BF16)

    own_columns = onehot(column_index - row_index == left_column)
    placed = [[dot(grads[0, c], own_columns).astype(BF16)] for c in range(2)]

    corner_copy.wait_recv()
    for part in range(CHUNKS):
        grad_copy(part).wait_recv()
    peer_row = corners[1, 0:1, :]
    peer_columns = onehot(column_index - row_index == corners[1, 8:9, 0:columns])
    for c in range(2):
        placed[c].append(dot(grads[1, c], peer_columns).astype(BF16))

    strip_row = lax.broadcasted_iota(jnp.int32, (rows, side), 0)
    patch_row = lax.broadcasted_iota(jnp.int32, (rows, side), 1)
    distance = strip_row - patch_row

    def strip_part(owner, c):
        shifted = distance + owner * rows
        own_rows = onehot(shifted == top_row)
        peer_rows = onehot(shifted == peer_row)
        return dot(own_rows, placed[c][0]) + dot(peer_rows, placed[c][1])

    def strip(owner):
        return [strip_part(owner, c) for c in range(2)]

    def direct_copy(mask, c):
        place = mask - 1 if c == 0 else probe_count - 1
        return pltpu.make_async_remote_copy(
            src_ref=direct_out.at[place],
            dst_ref=direct_in.at[place],
            send_sem=direct_sems.at[0, place],
            recv_sem=direct_sems.at[1, place],
            device_id={"probe": flip(probe, mask, probe_count)},
            device_id_type=MESH,
        )

    def pair_copy(place):
        return pltpu.make_async_remote_copy(
            src_ref=pair_out.at[place],
            dst_ref=pair_in.at[place],
            send_sem=pair_sems.at[0, place],
            recv_sem=pair_sems.at[1, place],
            device_id={"probe": flip(probe, 1, probe_count)},
            device_id_type=MESH,
        )

    def sum_copy(place):
        return pltpu.make_async_remote_copy(
            src_ref=sum_out.at[place],
            dst_ref=sum_in.at[place],
            send_sem=sum_sems.at[0, place],
            recv_sem=sum_sems.at[1, place],
            device_id={"probe": flip(probe, 2 * place + 2, probe_count)},
            device_id_type=MESH,
        )

    others = range(probe_count // 2 - 1, 0, -1)
    for other in others:
        mask = 2 * other + 1
        owner = flip(probe, mask, probe_count)
        pair_out[other - 1] = strip_part(owner, 1).astype(BF16)
        pair_copy(other - 1).start()
        direct_out[mask - 1] = strip_part(owner, 0).astype(BF16)
        direct_copy(mask, 0).start()
    for other in others:
        mask = 2 * other
        real, imag = strip(flip(probe, mask, probe_count))
        direct_out[mask - 1] = real.astype(BF16)
        direct_copy(mask, 0).start()
        held[other - 1] = imag
    real, imag = strip(flip(probe, 1, probe_count))
    direct_out[0] = real.astype(BF16)
    direct_out[probe_count - 1] = imag.astype(BF16)
    direct_copy(1, 0).start()
    direct_copy(1, 1).start()
    for other in others:
        pair_copy(other - 1).wait_recv()
        sum_out[other - 1] = (held[other - 1] + pair_in[other - 1].astype(F32)).astype(BF16)
        sum_copy(other - 1).start()
    total = strip(probe)
    for c in range(2):
        out[c, 0] = total[c]
    for mask in range(probe_count - 1, 0, -1):
        direct_copy(mask, 0).wait_recv()
        out[0, 0] += direct_in[mask - 1].astype(F32)
    direct_copy(1, 1).wait_recv()
    out[1, 0] += direct_in[probe_count - 1].astype(F32)
    for other in others:
        sum_copy(other - 1).wait_recv()
        out[1, 0] += sum_in[other - 1].astype(F32)

    corner_copy.wait_send()
    for part in range(CHUNKS):
        grad_copy(part).wait_send()
    for mask in range(1, probe_count):
        direct_copy(mask, 0).wait_send()
    direct_copy(1, 1).wait_send()
    for other in others:
        pair_copy(other - 1).wait_send()
        sum_copy(other - 1).wait_send()

    @pl.when(has_below)
    def _():
        for part in range(CHUNKS):
            hand_copy(part).wait_send()


def rolled_kernel(
    kept,
    top_modes,
    bottom_modes,
    top_order,
    bottom_order,
    waves_hbm,
    layers_hbm,
    residual_hbm,
    offsets_hbm,
    slot,
    table_hbm,
    out,
    waves,
    layers,
    residual,
    table,
    offsets,
    left_table,
    right_table,
    hand_out,
    hand_in,
    rolled,
    rolled_in,
    grads,
    grads_in,
    near_in,
    far_in,
    near_out,
    far_out,
    masks,
    near_masks,
    corners,
    mid_out,
    mid_in,
    own_out,
    own_in,
    load_sems,
    send_sems,
    hand_sems,
    rolled_sems,
    corner_sems,
    tile_sems,
    near_sems,
    aux_sems,
    mid_sems,
    own_sems,
    ready_sems,
):
    side = waves.shape[-1]
    rows = out.shape[2]
    step = rolled.shape[2]
    units = side // step
    chunks = rows // step
    depth = lax.axis_index("depth")
    probe = lax.axis_index("probe")
    tile = lax.axis_index("tile")
    is_top = depth == 1
    is_bottom = depth == 0
    block = probe % 2
    half = probe // 2

    def at_probe(mask):
        return flip(probe, mask, 4)

    barrier = pltpu.get_barrier_semaphore()

    def greet(device):
        pl.semaphore_signal(barrier, inc=1, device_id=device, device_id_type=MESH)

    greet({"depth": 1 - depth, "tile": 0})
    greet({"tile": 1 - tile})
    for mask in range(1, 4):
        greet({"probe": at_probe(mask), "tile": 1})

    @pl.when(is_bottom)
    def _():
        for mask in range(1, 4):
            greet({"probe": at_probe(mask), "depth": 1, "tile": 1})

    def wait_depth():
        @pl.when(tile == 0)
        def _():
            pl.semaphore_wait(barrier, 3)
            pl.semaphore_signal(ready_sems.at[0], inc=1, device_id={"tile": 1}, device_id_type=MESH)

        @pl.when(tile == 1)
        def _():
            pl.semaphore_wait(ready_sems.at[0], 1)

    def wait_probe(count):
        @pl.when(tile == 1)
        def _():
            pl.semaphore_wait(barrier, count)
            pl.semaphore_signal(ready_sems.at[1], inc=1, device_id={"tile": 0}, device_id_type=MESH)

        @pl.when(tile == 0)
        def _():
            pl.semaphore_wait(ready_sems.at[1], 1)

    load_offsets = pltpu.make_async_copy(offsets_hbm, offsets, load_sems.at[4])
    load_residual = pltpu.make_async_copy(residual_hbm, residual, load_sems.at[0])
    load_layers = pltpu.make_async_copy(layers_hbm, layers, load_sems.at[1])
    load_waves = pltpu.make_async_copy(waves_hbm, waves, load_sems.at[2])
    load_table = pltpu.make_async_copy(table_hbm, table, load_sems.at[3])
    load_offsets.start()

    @pl.when(is_top)
    def _():
        load_table.start()
        load_residual.start()
        load_layers.start()
        load_waves.start()

    @pl.when(is_bottom)
    def _():
        load_waves.start()
        load_table.start()

    load_offsets.wait()
    own_slot = slot[0]
    top_row = offsets[0, own_slot]
    left_column = offsets[1, own_slot]

    def onehot(match):
        return jnp.where(match, 1.0, 0.0).astype(BF16)

    row = lax.broadcasted_iota(jnp.int32, (side, side), 0)
    column = lax.broadcasted_iota(jnp.int32, (side, side), 1)
    row_move = onehot(column == ((row - top_row) & (side - 1)))
    column_move = onehot(row == ((column - left_column) & (side - 1)))

    def roll(value):
        return dot(dot(row_move, value).astype(BF16), column_move).astype(BF16)

    def roll_right_table():
        row_back = onehot(column == ((row + left_column) & (side - 1)))
        for part in range(2):
            right_table[part] = dot(row_back, table[part]).astype(BF16)

    kinds = ("hand", "rolled", "corner", "tile", "near", "aux", "mid", "own")

    def remote(kind, source, target, received, device):
        return pltpu.make_async_remote_copy(
            src_ref=source,
            dst_ref=target,
            send_sem=send_sems.at[kinds.index(kind)],
            recv_sem=received,
            device_id=device,
            device_id_type=MESH,
        )

    def unit_of(job):
        return job if job < units else kept[job - units]

    def place_of(job):
        return job % chunks if job < units else chunks + job - units

    def hand_copy(unit):
        return remote("hand", hand_out.at[unit], hand_in.at[unit], hand_sems.at[unit], {"depth": 0})

    def rolled_copy(place):
        source = rolled.at[kept[place]]
        return remote("rolled", source, rolled_in.at[place], rolled_sems.at[place], {"depth": 1})

    def corner_copy(place):
        device = [None, {"tile": 1 - tile}, {"probe": at_probe(1)}, {"probe": at_probe(1), "tile": 1 - tile}]
        return remote("corner", corners.at[0], corners.at[place], corner_sems.at[place - 1], device[place])

    def tile_copy(job):
        return remote("tile", grads.at[job], grads_in.at[job], tile_sems.at[job], {"tile": 1 - tile})

    def leave(job, mask):
        device = {"probe": at_probe(mask)} if mask else {}
        if job >= units:
            device["depth"] = 0
        return device

    def near_copy(job, direct):
        source, device = (near_out, leave(job, 1)) if direct else (grads, {"probe": at_probe(1)})
        return remote("near", source.at[job], near_in.at[0, job], near_sems.at[place_of(job)], device)

    def wide_copy(job):
        device = {"probe": at_probe(1), "tile": 1 - tile}
        return remote("aux", grads.at[job], near_in.at[1, job], aux_sems.at[place_of(job)], device)

    def far_copy(job):
        return remote("aux", far_out.at[job], far_in.at[job], aux_sems.at[place_of(job)], leave(job, 3))

    def pass_copy(job):
        source = near_in.at[0, job]
        return remote("aux", source, near_in.at[1, job], aux_sems.at[place_of(job)], {"tile": 1 - tile})

    def mid_copy(job):
        return remote("mid", mid_out.at[job], mid_in.at[job], mid_sems.at[place_of(job)], leave(job, 2))

    def own_copy(job):
        place = job - units
        return remote("own", own_out.at[place], own_in.at[place], own_sems.at[place], leave(job, 0))

    def wait_sent(kind, source, count):
        if count:
            remote(kind, source.at[0:count], source.at[0:count], corner_sems.at[0], {"tile": 1 - tile}).wait_send()

    def fill_corners():
        corners[0, 0:8, :] = jnp.full((8, side), top_row, jnp.int32)
        corners[0, 8:16, :] = jnp.full((8, side), left_column, jnp.int32)

    def make_masks(target, place, count, first):
        local_row = lax.broadcasted_iota(jnp.int32, (step, side), 0) + first
        local_column = lax.broadcasted_iota(jnp.int32, (step, side), 1)
        keep = (1 - tile).astype(F32)
        mine = jnp.where(local_column >= corners[place, 8:9, :], keep, 1.0 - keep)
        for unit in range(count):
            upper = jnp.where(local_row + unit * step >= corners[place, 0:1, :], mine, 0.0)
            target[place % 2, 0, unit] = upper.astype(BF16)
            target[place % 2, 1, unit] = (mine - upper).astype(BF16)

    def right_product(arrived):
        product = dot(arrived, right_table[0]) + dot(arrived, right_table[1])
        real = product[:step, :side] - product[step:, side:]
        imag = product[:step, side:] + product[step:, :side]
        return real, imag

    def put_gradient(job, gradient):
        for c in range(2):
            grads[job, c] = gradient[c].astype(BF16)

    def window_of(job):
        return pl.ds(unit_of(job) % chunks * step, step)

    def keeps(job):
        return block == unit_of(job) // chunks

    def gives(job):
        return block != unit_of(job) // chunks

    def strip(job, which, c, near):
        sources = [(grads, masks.at[0]), (grads_in, masks.at[1])]
        total = None
        for value, mask in sources:
            term = value[job, c].astype(F32) * mask[which, unit_of(job)].astype(F32)
            total = term if total is None else total + term
        for place in range(2 if near else 0):
            mask = near_masks[place, which, unit_of(job) % chunks].astype(F32)
            total = total + near_in[place, job, c].astype(F32) * mask
        return total

    def keep_strips(job, near):
        for c in range(2):
            mid_out[job, c] = strip(job, 1 - half, c, near).astype(BF16)
        mid_copy(job).start()
        for c in range(2):
            value = strip(job, half, c, near)
            if job < units:
                out[c, 0, window_of(job), :] = value
            else:
                own_out[job - units, c] = value.astype(BF16)
        if job >= units:
            own_copy(job).start()

    def stage_sum(job):
        @pl.when(keeps(job))
        def _():
            tile_copy(job).wait_recv()
            pass_copy(job).wait_recv()
            keep_strips(job, True)

    def stage_wide(job):
        @pl.when(keeps(job))
        def _():
            tile_copy(job).wait_recv()
            near_copy(job, False).wait_recv()
            wide_copy(job).wait_recv()
            keep_strips(job, True)

    def stage_direct(job):
        tile_copy(job).wait_recv()

        @pl.when(gives(job))
        def _():
            for c in range(2):
                far_out[job, c] = strip(job, 1 - half, c, False).astype(BF16)
            far_copy(job).start()
            for c in range(2):
                near_out[job, c] = strip(job, half, c, False).astype(BF16)
            near_copy(job, True).start()

        @pl.when(keeps(job))
        def _():
            keep_strips(job, False)

    def stage_pass(job):
        @pl.when(keeps(job))
        def _():
            near_copy(job, False).wait_recv()
            pass_copy(job).start()

    def stage_add(job, direct):
        @pl.when(keeps(job))
        def _():
            if job < units:
                first = [out[c, 0, window_of(job), :] for c in range(2)]
            else:
                own_copy(job).wait_recv()
                first = [own_in[job - units, c].astype(F32) for c in range(2)]
            if direct:
                near_copy(job, True).wait_recv()
                far_copy(job).wait_recv()
            mid_copy(job).wait_recv()
            for c in range(2):
                total = first[c] + mid_in[job, c].astype(F32)
                if direct:
                    total = total + near_in[0, job, c].astype(F32) + far_in[job, c].astype(F32)
                out[c, 0, window_of(job), :] = total

    def stage_masks(place):
        if place > 0:
            corner_copy(place).wait_recv()
        if place < 2:
            make_masks(masks, place, units, 0)
        else:
            make_masks(near_masks, place, chunks, block * rows)

    def send(job, mode):
        if mode == "d":
            tile_copy(job).start()
        else:

            @pl.when(keeps(job))
            def _():
                tile_copy(job).start()

            @pl.when(gives(job))
            def _():
                near_copy(job, False).start()
                if mode == "w":
                    wide_copy(job).start()

    def finish(jobs, modes):
        for half_units in range(2):
            count = dict.fromkeys(kinds, 0)
            for job in jobs:
                own_half = unit_of(job) // chunks == half_units
                mode = modes[job]
                count["tile"] += own_half or mode == "d"
                count["mid"] += own_half
                count["own"] += own_half and job >= units
                count["near"] += not own_half
                count["aux"] += mode == "r" if own_half else mode != "r"

            @pl.when(block == half_units)
            def _():
                wait_sent("tile", grads, count["tile"])
                wait_sent("near", grads, count["near"])
                wait_sent("aux", grads, count["aux"])
                wait_sent("mid", mid_out, count["mid"])
                wait_sent("own", own_out, count["own"])

    def run(order, modes, jobs, stage_gradient):
        stages = dict(
            g=stage_gradient,
            m=stage_masks,
            d=stage_direct,
            p=stage_pass,
            s=stage_sum,
            w=stage_wide,
            a=lambda job: stage_add(job, (top_modes if job >= units else modes)[job] == "d"),
        )
        for kind, number in order:
            stages[kind](number)
        wait_sent("corner", corners, 3)
        finish(jobs, modes)

    @pl.when(is_top)
    def _():
        fill_corners()
        load_table.wait()
        for part in range(2):
            product = dot(row_move, table[part]).astype(BF16)
            for unit in range(units):
                for c in range(2):
                    left_table[unit, 2 * part + c] = product[
                        unit * step : (unit + 1) * step, c * side : (c + 1) * side
                    ]
        load_residual.wait()
        load_layers.wait()
        handed = conj_times(
            layers[0, 0, 0].astype(F32), layers[0, 0, 1].astype(F32), residual[0, 0], residual[0, 1]
        )
        handed = jnp.concatenate([handed[0].astype(BF16), handed[1].astype(BF16)], axis=1)
        first = True
        for unit in [number for kind, number in bottom_order if kind == "g"] + list(kept):
            product = dot(left_table[unit].reshape(4 * step, side), handed)
            by_real = product[:step] + product[2 * step : 3 * step]
            by_imag = product[step : 2 * step] + product[3 * step :]
            hand_out[unit, 0] = (by_real[:, :side] - by_imag[:, side:]).astype(BF16)
            hand_out[unit, 1] = (by_real[:, side:] + by_imag[:, :side]).astype(BF16)
            if first:
                wait_depth()
                first = False
            if unit not in kept:
                hand_copy(unit).start()
        corner_copy(1).start()
        load_waves.wait()
        gradient = conj_times(
            waves[0, 0, 0].astype(F32), waves[0, 0, 1].astype(F32), residual[0, 0], residual[0, 1]
        )
        gradient = [roll(gradient[c].astype(BF16)) for c in range(2)]
        for unit in range(units):
            put_gradient(unit, [gradient[c][unit * step : (unit + 1) * step] for c in range(2)])
        wait_probe(13)
        corner_copy(2).start()
        corner_copy(3).start()

        def stage_gradient(job):
            if job == units:
                roll_right_table()
            if job >= units:
                real, imag = right_product(hand_out[unit_of(job)].reshape(2 * step, side))
                rolled_copy(job - units).wait_recv()
                source = rolled_in[job - units].astype(F32)
                put_gradient(job, conj_times(source[0], source[1], real, imag))
            send(job, top_modes[job])

        run(top_order, top_modes, range(units + len(kept)), stage_gradient)
        wait_sent("hand", hand_out, units - len(kept))

    @pl.when(is_bottom)
    def _():
        fill_corners()
        load_waves.wait()
        source = [roll(waves[0, 0, c]) for c in range(2)]
        for unit in range(units):
            for c in range(2):
                rolled[unit, c] = source[c][unit * step : (unit + 1) * step]
        wait_depth()
        for place in range(len(kept)):
            rolled_copy(place).start()
        corner_copy(1).start()
        load_table.wait()
        roll_right_table()
        wait_probe(7)
        corner_copy(2).start()
        corner_copy(3).start()

        def stage_gradient(job):
            hand_copy(job).wait_recv()
            real, imag = right_product(hand_in[job].reshape(2 * step, side))
            source = rolled[job].astype(F32)
            put_gradient(job, conj_times(source[0], source[1], real, imag))
            send(job, bottom_modes[job])

        jobs = [unit for unit in range(units) if unit not in kept]
        run(bottom_order, bottom_modes, jobs, stage_gradient)
        wait_sent("rolled", rolled, len(kept))


def orders(text):
    return [(step[0], int(step[1:])) for step in text]


def rolled_call(waves, layers, residual, offsets, slot, rows, columns, step, kept, top, bottom):
    side = waves.shape[-1]
    table = propagator(side)
    units = side // step
    jobs = units + len(kept)
    hbm = pl.BlockSpec(memory_space=pltpu.HBM)

    def copies(count):
        return pltpu.SemaphoreType.DMA((count,))

    return pl.pallas_call(
        functools.partial(rolled_kernel, kept, top, bottom, orders(TOP_STEPS), orders(BOTTOM_STEPS)),
        out_shape=jax.ShapeDtypeStruct((2, 1, rows, columns), F32),
        in_specs=[hbm] * 4 + [pl.BlockSpec(memory_space=pltpu.SMEM), hbm],
        out_specs=pl.BlockSpec(memory_space=pltpu.VMEM),
        scratch_shapes=[
            pltpu.VMEM(waves.shape, waves.dtype),
            pltpu.VMEM(layers.shape, layers.dtype),
            pltpu.VMEM(residual.shape, residual.dtype),
            pltpu.VMEM(table.shape, BF16),
            pltpu.SMEM(offsets.shape[::-1], jnp.int32),
            pltpu.VMEM((units, 4, step, side), BF16),
            pltpu.VMEM(table.shape, BF16),
            pltpu.VMEM((units, 2, step, side), BF16),
            pltpu.VMEM((units, 2, step, side), BF16),
            pltpu.VMEM((units, 2, step, side), BF16),
            pltpu.VMEM((max(len(kept), 1), 2, step, side), BF16),
            pltpu.VMEM((jobs, 2, step, side), BF16),
            pltpu.VMEM((jobs, 2, step, side), BF16),
            pltpu.VMEM((2, jobs, 2, step, side), BF16),
            pltpu.VMEM((jobs, 2, step, side), BF16),
            pltpu.VMEM((jobs, 2, step, side), BF16),
            pltpu.VMEM((jobs, 2, step, side), BF16),
            pltpu.VMEM((2, 2, units, step, side), BF16),
            pltpu.VMEM((2, 2, rows // step, step, side), BF16),
            pltpu.VMEM((4, 16, side), jnp.int32),
            pltpu.VMEM((jobs, 2, step, columns), BF16),
            pltpu.VMEM((jobs, 2, step, columns), BF16),
            pltpu.VMEM((max(len(kept), 1), 2, step, columns), BF16),
            pltpu.VMEM((max(len(kept), 1), 2, step, columns), BF16),
            pltpu.SemaphoreType.DMA((5,)),
            copies(8),
            copies(units),
            copies(max(len(kept), 1)),
            copies(3),
            copies(jobs),
            copies(rows // step + len(kept)),
            copies(rows // step + len(kept)),
            copies(rows // step + len(kept)),
            copies(max(len(kept), 1)),
            pltpu.SemaphoreType.REGULAR((2,)),
        ],
        compiler_params=pltpu.CompilerParams(
            collective_id=0, has_side_effects=True, vmem_limit_bytes=32 * 1024 * 1024
        ),
    )(
        *(pltpu.with_memory_space_constraint(x, pltpu.HBM) for x in (waves, layers, residual, offsets.T)),
        slot,
        pltpu.with_memory_space_constraint(jnp.asarray(table), pltpu.HBM),
    )


def per_device(depth_count, probe_count, tile_count, waves, layers, residual, offsets, slot):
    side = waves.shape[-1]
    rows, columns = OBJ // probe_count, OBJ // tile_count
    if (depth_count, probe_count, tile_count) == (2, 4, 2) and OBJ == 2 * side:
        return rolled_call(
            waves, layers, residual, offsets, slot, rows, columns, 32, KEPT, TOP_MODES, BOTTOM_MODES
        )
    table = propagator(side)
    others = probe_count // 2 - 1
    vmem = pl.BlockSpec(memory_space=pltpu.VMEM)
    smem = pl.BlockSpec(memory_space=pltpu.SMEM)
    hbm = pl.BlockSpec(memory_space=pltpu.HBM)
    return pl.pallas_call(
        functools.partial(kernel, depth_count, probe_count),
        out_shape=jax.ShapeDtypeStruct((2, 1, rows, columns), F32),
        in_specs=[hbm, hbm, hbm, smem, smem, hbm],
        out_specs=vmem,
        scratch_shapes=[
            pltpu.VMEM(waves.shape, waves.dtype),
            pltpu.VMEM(layers.shape, layers.dtype),
            pltpu.VMEM(residual.shape, residual.dtype),
            pltpu.VMEM(table.shape, BF16),
            pltpu.VMEM((2, side, side), BF16),
            pltpu.VMEM((2, side, side), BF16),
            pltpu.VMEM((side, 2 * side), BF16),
            pltpu.VMEM((2, 2, side, side), BF16),
            pltpu.VMEM((2, 16, side), jnp.int32),
            pltpu.VMEM((probe_count, rows, columns), BF16),
            pltpu.VMEM((probe_count, rows, columns), BF16),
            pltpu.VMEM((others, rows, columns), BF16),
            pltpu.VMEM((others, rows, columns), BF16),
            pltpu.VMEM((others, rows, columns), BF16),
            pltpu.VMEM((others, rows, columns), BF16),
            pltpu.VMEM((others, rows, columns), F32),
            pltpu.SemaphoreType.DMA((4,)),
            pltpu.SemaphoreType.DMA((2, CHUNKS)),
            pltpu.SemaphoreType.DMA((2, CHUNKS)),
            pltpu.SemaphoreType.DMA((2,)),
            pltpu.SemaphoreType.DMA((2, probe_count)),
            pltpu.SemaphoreType.DMA((2, others)),
            pltpu.SemaphoreType.DMA((2, others)),
        ],
        compiler_params=pltpu.CompilerParams(
            collective_id=0, has_side_effects=True, vmem_limit_bytes=32 * 1024 * 1024
        ),
    )(
        *(pltpu.with_memory_space_constraint(x, pltpu.HBM) for x in (waves, layers, residual)),
        offsets.T,
        slot,
        pltpu.with_memory_space_constraint(jnp.asarray(table), pltpu.HBM),
    )


def solution(mesh):
    return jax.shard_map(
        functools.partial(per_device, mesh.shape["depth"], mesh.shape["probe"], mesh.shape["tile"]),
        mesh=mesh,
        in_specs=(
            P("depth", ("groups", "probe", "tile"), None, None, None),
            P("depth", ("groups", "probe", "tile"), None, None, None),
            P(("groups", "probe", "tile"), None, None, None),
            P("groups", None),
            P(("groups", "probe", "tile")),
        ),
        out_specs=P("groups", "depth", "probe", "tile"),
        check_vma=False,
    )
```

```python
import functools

import jax
import jax.numpy as jnp
import ml_dtypes
import numpy as np
from jax import lax
from jax.experimental import pallas as pl
from jax.experimental.pallas import tpu as pltpu
from jax.sharding import PartitionSpec as P

OBJ = 512
CHUNKS = 1
MESH = pl.DeviceIdType.MESH
F32 = jnp.float32
BF16 = jnp.bfloat16
KEPT = (6, 7)
TOP_MODES = ('d', 'd', 'd', 'w', 'r', 'r', 'r', 'd', 'r', 'w')
BOTTOM_MODES = ('r', 'r', 'd', 'd', 'r', 'w', 'r', 'r')
TOP_STEPS = ['g3', 'g0', 'g1', 'g2', 'g4', 'g5', 'g6', 'g7', 'g8', 'm0', 'm1', 'd0', 'd1', 'd2', 'd7', 'g9', 'p4', 'm2', 'm3', 'w3', 'p5', 'p8', 's4', 'p6', 's5', 's8', 'w9', 's6', 'a0', 'a1', 'a2', 'a7', 'a3', 'a4', 'a5', 'a6']
BOTTOM_STEPS = ['m0', 'm1', 'g0', 'g2', 'g1', 'd2', 'g3', 'g4', 'p0', 'd3', 'g5', 'm2', 'm3', 's0', 'p1', 's1', 'p4', 's4', 'w5', 'a2', 'a3', 'a9', 'a0', 'a8', 'a1', 'a4', 'a5']


def propagator(side):
    counter = np.arange(side)
    frequency = (counter + side // 2) % side - side // 2
    chirp = np.exp(0.5j * frequency.astype(np.float64) ** 2 / side)
    column = np.fft.ifft(chirp)
    matrix = column[(counter[:, None] - counter[None, :]) % side]
    parts = np.concatenate([matrix.real, matrix.imag], axis=1)
    high = parts.astype(ml_dtypes.bfloat16)
    low = (parts - high.astype(np.float64)).astype(ml_dtypes.bfloat16)
    return np.stack([high, low])


def dot(a, b):
    return jnp.dot(a, b, preferred_element_type=F32)


def split(value):
    high = value.astype(BF16)
    return high, (value - high.astype(F32)).astype(BF16)


def conj_times(layer_real, layer_imag, real, imag):
    return (
        layer_real * real + layer_imag * imag,
        layer_real * imag - layer_imag * real,
    )


def flip(index, mask, count):
    result, bit = 0, 1
    while bit < count:
        result = result + ((index // bit + (mask // bit) % 2) % 2) * bit
        bit *= 2
    return result


def kernel(
    depth_count,
    probe_count,
    waves_hbm,
    layers_hbm,
    residual_hbm,
    offsets,
    slot,
    table_hbm,
    out,
    waves,
    layers,
    residual,
    table,
    hand_out,
    hand_in,
    turned,
    grads,
    corners,
    direct_out,
    direct_in,
    pair_out,
    pair_in,
    sum_out,
    sum_in,
    held,
    load_sems,
    hand_sems,
    grad_sems,
    corner_sems,
    direct_sems,
    pair_sems,
    sum_sems,
):
    side = waves.shape[-1]
    rows, columns = out.shape[2], out.shape[3]
    step = side // CHUNKS
    depth = lax.axis_index("depth")
    probe = lax.axis_index("probe")
    tile = lax.axis_index("tile")
    is_top = depth == depth_count - 1
    has_below = depth > 0

    barrier = pltpu.get_barrier_semaphore()
    for mask in range(1, probe_count):
        pl.semaphore_signal(
            barrier, inc=1, device_id={"probe": flip(probe, mask, probe_count)}, device_id_type=MESH
        )
    pl.semaphore_signal(barrier, inc=1, device_id={"tile": 1 - tile}, device_id_type=MESH)

    @pl.when(depth < depth_count - 1)
    def _():
        pl.semaphore_signal(barrier, inc=1, device_id={"depth": depth + 1}, device_id_type=MESH)

    load_residual = pltpu.make_async_copy(residual_hbm, residual, load_sems.at[0])
    load_layers = pltpu.make_async_copy(layers_hbm, layers, load_sems.at[1])
    load_waves = pltpu.make_async_copy(waves_hbm, waves, load_sems.at[2])
    load_table = pltpu.make_async_copy(table_hbm, table, load_sems.at[3])

    @pl.when(is_top)
    def _():
        load_residual.start()

    if depth_count > 1:

        @pl.when(has_below)
        def _():
            load_layers.start()

        @pl.when(jnp.logical_not(is_top))
        def _():
            load_table.start()

    load_waves.start()

    own_slot = slot[0]
    top_row = offsets[0, own_slot]
    left_column = offsets[1, own_slot]
    corners[0, 0:8, :] = jnp.full((8, side), top_row, jnp.int32)
    corners[0, 8:16, :] = jnp.full((8, side), left_column, jnp.int32)

    @pl.when(has_below)
    def _():
        pl.semaphore_wait(barrier, probe_count + 1)

    @pl.when(jnp.logical_not(has_below))
    def _():
        pl.semaphore_wait(barrier, probe_count)

    corner_copy = pltpu.make_async_remote_copy(
        src_ref=corners.at[0],
        dst_ref=corners.at[1],
        send_sem=corner_sems.at[0],
        recv_sem=corner_sems.at[1],
        device_id={"tile": 1 - tile},
        device_id_type=MESH,
    )
    corner_copy.start()

    def hand_copy(part):
        window = pl.ds(part * step, step)
        return pltpu.make_async_remote_copy(
            src_ref=hand_out.at[:, window, :],
            dst_ref=hand_in.at[:, window, :],
            send_sem=hand_sems.at[0, part],
            recv_sem=hand_sems.at[1, part],
            device_id={"depth": depth - 1},
            device_id_type=MESH,
        )

    def grad_copy(part):
        window = pl.ds(part * step, step)
        return pltpu.make_async_remote_copy(
            src_ref=grads.at[0, :, window, :],
            dst_ref=grads.at[1, :, window, :],
            send_sem=grad_sems.at[0, part],
            recv_sem=grad_sems.at[1, part],
            device_id={"tile": 1 - tile},
            device_id_type=MESH,
        )

    def hand_down(part, real, imag):
        window = pl.ds(part * step, step)
        handed = conj_times(
            layers[0, 0, 0, window, :].astype(F32), layers[0, 0, 1, window, :].astype(F32), real, imag
        )
        hand_out[0, window, :] = handed[0].astype(BF16)
        hand_out[1, window, :] = handed[1].astype(BF16)
        hand_copy(part).start()

    def give_gradient(part, real, imag):
        window = pl.ds(part * step, step)
        gradient = conj_times(
            waves[0, 0, 0, window, :].astype(F32), waves[0, 0, 1, window, :].astype(F32), real, imag
        )
        grads[0, 0, window, :] = gradient[0].astype(BF16)
        grads[0, 1, window, :] = gradient[1].astype(BF16)
        grad_copy(part).start()

    @pl.when(is_top)
    def _():
        load_residual.wait()
        if depth_count > 1:
            load_layers.wait()
            for part in range(CHUNKS):
                window = pl.ds(part * step, step)
                hand_down(part, residual[0, 0, window, :], residual[0, 1, window, :])
        load_waves.wait()
        for part in range(CHUNKS):
            window = pl.ds(part * step, step)
            give_gradient(part, residual[0, 0, window, :], residual[0, 1, window, :])

    if depth_count > 1:

        @pl.when(jnp.logical_not(is_top))
        def _():
            load_table.wait()
            load_waves.wait()
            if depth_count > 2:

                @pl.when(has_below)
                def _():
                    load_layers.wait()

            for part in range(CHUNKS):
                window = pl.ds(part * step, step)
                hand_copy(part).wait_recv()
                real = dot(hand_in[0, window, :], table[0]) + dot(hand_in[0, window, :], table[1])
                imag = dot(hand_in[1, window, :], table[0]) + dot(hand_in[1, window, :], table[1])
                product = real[:, :side] - imag[:, side:], real[:, side:] + imag[:, :side]
                for c in range(2):
                    turned[window, pl.ds(c * side, side)] = product[c].astype(BF16)

            for part in range(CHUNKS):
                window = pl.ds(part * step, step)

                def from_left(index):
                    columns = pl.ds(index * side, side)
                    return (
                        dot(table[0, window, columns], turned[...]) + dot(table[1, window, columns], turned[...])
                    )

                by_real, by_imag = from_left(0), from_left(1)
                real = by_real[:, :side] - by_imag[:, side:]
                imag = by_real[:, side:] + by_imag[:, :side]
                if depth_count > 2:

                    @pl.when(has_below)
                    def _():
                        hand_down(part, real, imag)

                give_gradient(part, real, imag)

    row_index = lax.broadcasted_iota(jnp.int32, (side, columns), 0)
    column_index = lax.broadcasted_iota(jnp.int32, (side, columns), 1) + tile * columns

    def onehot(match):
        return jnp.where(match, 1.0, 0.0).astype(BF16)

    own_columns = onehot(column_index - row_index == left_column)
    placed = [[dot(grads[0, c], own_columns).astype(BF16)] for c in range(2)]

    corner_copy.wait_recv()
    for part in range(CHUNKS):
        grad_copy(part).wait_recv()
    peer_row = corners[1, 0:1, :]
    peer_columns = onehot(column_index - row_index == corners[1, 8:9, 0:columns])
    for c in range(2):
        placed[c].append(dot(grads[1, c], peer_columns).astype(BF16))

    strip_row = lax.broadcasted_iota(jnp.int32, (rows, side), 0)
    patch_row = lax.broadcasted_iota(jnp.int32, (rows, side), 1)
    distance = strip_row - patch_row

    def strip_part(owner, c):
        shifted = distance + owner * rows
        own_rows = onehot(shifted == top_row)
        peer_rows = onehot(shifted == peer_row)
        return dot(own_rows, placed[c][0]) + dot(peer_rows, placed[c][1])

    def strip(owner):
        return [strip_part(owner, c) for c in range(2)]

    def direct_copy(mask, c):
        place = mask - 1 if c == 0 else probe_count - 1
        return pltpu.make_async_remote_copy(
            src_ref=direct_out.at[place],
            dst_ref=direct_in.at[place],
            send_sem=direct_sems.at[0, place],
            recv_sem=direct_sems.at[1, place],
            device_id={"probe": flip(probe, mask, probe_count)},
            device_id_type=MESH,
        )

    def pair_copy(place):
        return pltpu.make_async_remote_copy(
            src_ref=pair_out.at[place],
            dst_ref=pair_in.at[place],
            send_sem=pair_sems.at[0, place],
            recv_sem=pair_sems.at[1, place],
            device_id={"probe": flip(probe, 1, probe_count)},
            device_id_type=MESH,
        )

    def sum_copy(place):
        return pltpu.make_async_remote_copy(
            src_ref=sum_out.at[place],
            dst_ref=sum_in.at[place],
            send_sem=sum_sems.at[0, place],
            recv_sem=sum_sems.at[1, place],
            device_id={"probe": flip(probe, 2 * place + 2, probe_count)},
            device_id_type=MESH,
        )

    others = range(probe_count // 2 - 1, 0, -1)
    for other in others:
        mask = 2 * other + 1
        owner = flip(probe, mask, probe_count)
        pair_out[other - 1] = strip_part(owner, 1).astype(BF16)
        pair_copy(other - 1).start()
        direct_out[mask - 1] = strip_part(owner, 0).astype(BF16)
        direct_copy(mask, 0).start()
    for other in others:
        mask = 2 * other
        real, imag = strip(flip(probe, mask, probe_count))
        direct_out[mask - 1] = real.astype(BF16)
        direct_copy(mask, 0).start()
        held[other - 1] = imag
    real, imag = strip(flip(probe, 1, probe_count))
    direct_out[0] = real.astype(BF16)
    direct_out[probe_count - 1] = imag.astype(BF16)
    direct_copy(1, 0).start()
    direct_copy(1, 1).start()
    for other in others:
        pair_copy(other - 1).wait_recv()
        sum_out[other - 1] = (held[other - 1] + pair_in[other - 1].astype(F32)).astype(BF16)
        sum_copy(other - 1).start()
    total = strip(probe)
    for c in range(2):
        out[c, 0] = total[c]
    for mask in range(probe_count - 1, 0, -1):
        direct_copy(mask, 0).wait_recv()
        out[0, 0] += direct_in[mask - 1].astype(F32)
    direct_copy(1, 1).wait_recv()
    out[1, 0] += direct_in[probe_count - 1].astype(F32)
    for other in others:
        sum_copy(other - 1).wait_recv()
        out[1, 0] += sum_in[other - 1].astype(F32)

    corner_copy.wait_send()
    for part in range(CHUNKS):
        grad_copy(part).wait_send()
    for mask in range(1, probe_count):
        direct_copy(mask, 0).wait_send()
    direct_copy(1, 1).wait_send()
    for other in others:
        pair_copy(other - 1).wait_send()
        sum_copy(other - 1).wait_send()

    @pl.when(has_below)
    def _():
        for part in range(CHUNKS):
            hand_copy(part).wait_send()


def rolled_kernel(
    kept,
    top_modes,
    bottom_modes,
    top_order,
    bottom_order,
    waves_hbm,
    layers_hbm,
    residual_hbm,
    offsets_hbm,
    slot,
    table_hbm,
    out,
    waves,
    layers,
    residual,
    table,
    offsets,
    left_table,
    right_table,
    hand_out,
    hand_in,
    rolled,
    rolled_in,
    grads,
    grads_in,
    near_in,
    far_in,
    near_out,
    far_out,
    masks,
    near_masks,
    corners,
    mid_out,
    mid_in,
    own_out,
    own_in,
    load_sems,
    send_sems,
    hand_sems,
    rolled_sems,
    corner_sems,
    tile_sems,
    near_sems,
    aux_sems,
    mid_sems,
    own_sems,
    ready_sems,
):
    side = waves.shape[-1]
    rows = out.shape[2]
    step = rolled.shape[2]
    units = side // step
    chunks = rows // step
    depth = lax.axis_index("depth")
    probe = lax.axis_index("probe")
    tile = lax.axis_index("tile")
    is_top = depth == 1
    is_bottom = depth == 0
    block = probe % 2
    half = probe // 2

    def at_probe(mask):
        return flip(probe, mask, 4)

    barrier = pltpu.get_barrier_semaphore()

    def greet(device):
        pl.semaphore_signal(barrier, inc=1, device_id=device, device_id_type=MESH)

    greet({"depth": 1 - depth, "tile": 0})
    greet({"tile": 1 - tile})
    for mask in range(1, 4):
        greet({"probe": at_probe(mask), "tile": 1})

    @pl.when(is_bottom)
    def _():
        for mask in range(1, 4):
            greet({"probe": at_probe(mask), "depth": 1, "tile": 1})

    def wait_depth():
        @pl.when(tile == 0)
        def _():
            pl.semaphore_wait(barrier, 3)
            pl.semaphore_signal(ready_sems.at[0], inc=1, device_id={"tile": 1}, device_id_type=MESH)

        @pl.when(tile == 1)
        def _():
            pl.semaphore_wait(ready_sems.at[0], 1)

    def wait_probe(count):
        @pl.when(tile == 1)
        def _():
            pl.semaphore_wait(barrier, count)
            pl.semaphore_signal(ready_sems.at[1], inc=1, device_id={"tile": 0}, device_id_type=MESH)

        @pl.when(tile == 0)
        def _():
            pl.semaphore_wait(ready_sems.at[1], 1)

    load_offsets = pltpu.make_async_copy(offsets_hbm, offsets, load_sems.at[4])
    load_residual = pltpu.make_async_copy(residual_hbm, residual, load_sems.at[0])
    load_layers = pltpu.make_async_copy(layers_hbm, layers, load_sems.at[1])
    load_waves = pltpu.make_async_copy(waves_hbm, waves, load_sems.at[2])
    load_table = pltpu.make_async_copy(table_hbm, table, load_sems.at[3])
    load_offsets.start()

    @pl.when(is_top)
    def _():
        load_table.start()
        load_residual.start()
        load_layers.start()
        load_waves.start()

    @pl.when(is_bottom)
    def _():
        load_waves.start()
        load_table.start()

    load_offsets.wait()
    own_slot = slot[0]
    top_row = offsets[0, own_slot]
    left_column = offsets[1, own_slot]

    def onehot(match):
        return jnp.where(match, 1.0, 0.0).astype(BF16)

    row = lax.broadcasted_iota(jnp.int32, (side, side), 0)
    column = lax.broadcasted_iota(jnp.int32, (side, side), 1)
    row_move = onehot(column == ((row - top_row) & (side - 1)))
    column_move = onehot(row == ((column - left_column) & (side - 1)))

    def roll(value):
        return dot(dot(row_move, value).astype(BF16), column_move).astype(BF16)

    def roll_right_table():
        row_back = onehot(column == ((row + left_column) & (side - 1)))
        for part in range(2):
            right_table[part] = dot(row_back, table[part]).astype(BF16)

    kinds = ("hand", "rolled", "corner", "tile", "near", "aux", "mid", "own")

    def remote(kind, source, target, received, device):
        return pltpu.make_async_remote_copy(
            src_ref=source,
            dst_ref=target,
            send_sem=send_sems.at[kinds.index(kind)],
            recv_sem=received,
            device_id=device,
            device_id_type=MESH,
        )

    def unit_of(job):
        return job if job < units else kept[job - units]

    def place_of(job):
        return job % chunks if job < units else chunks + job - units

    def hand_copy(unit):
        return remote("hand", hand_out.at[unit], hand_in.at[unit], hand_sems.at[unit], {"depth": 0})

    def rolled_copy(place):
        source = rolled.at[kept[place]]
        return remote("rolled", source, rolled_in.at[place], rolled_sems.at[place], {"depth": 1})

    def corner_copy(place):
        device = [None, {"tile": 1 - tile}, {"probe": at_probe(1)}, {"probe": at_probe(1), "tile": 1 - tile}]
        return remote("corner", corners.at[0], corners.at[place], corner_sems.at[place - 1], device[place])

    def tile_copy(job):
        return remote("tile", grads.at[job], grads_in.at[job], tile_sems.at[job], {"tile": 1 - tile})

    def leave(job, mask):
        device = {"probe": at_probe(mask)} if mask else {}
        if job >= units:
            device["depth"] = 0
        return device

    def near_copy(job, direct):
        source, device = (near_out, leave(job, 1)) if direct else (grads, {"probe": at_probe(1)})
        return remote("near", source.at[job], near_in.at[0, job], near_sems.at[place_of(job)], device)

    def wide_copy(job):
        device = {"probe": at_probe(1), "tile": 1 - tile}
        return remote("aux", grads.at[job], near_in.at[1, job], aux_sems.at[place_of(job)], device)

    def far_copy(job):
        return remote("aux", far_out.at[job], far_in.at[job], aux_sems.at[place_of(job)], leave(job, 3))

    def pass_copy(job):
        source = near_in.at[0, job]
        return remote("aux", source, near_in.at[1, job], aux_sems.at[place_of(job)], {"tile": 1 - tile})

    def mid_copy(job):
        return remote("mid", mid_out.at[job], mid_in.at[job], mid_sems.at[place_of(job)], leave(job, 2))

    def own_copy(job):
        place = job - units
        return remote("own", own_out.at[place], own_in.at[place], own_sems.at[place], leave(job, 0))

    def wait_sent(kind, source, count):
        if count:
            remote(kind, source.at[0:count], source.at[0:count], corner_sems.at[0], {"tile": 1 - tile}).wait_send()

    def fill_corners():
        corners[0, 0:8, :] = jnp.full((8, side), top_row, jnp.int32)
        corners[0, 8:16, :] = jnp.full((8, side), left_column, jnp.int32)

    def make_masks(target, place, count, first):
        local_row = lax.broadcasted_iota(jnp.int32, (step, side), 0) + first
        local_column = lax.broadcasted_iota(jnp.int32, (step, side), 1)
        keep = (1 - tile).astype(F32)
        mine = jnp.where(local_column >= corners[place, 8:9, :], keep, 1.0 - keep)
        for unit in range(count):
            upper = jnp.where(local_row + unit * step >= corners[place, 0:1, :], mine, 0.0)
            target[place % 2, 0, unit] = upper.astype(BF16)
            target[place % 2, 1, unit] = (mine - upper).astype(BF16)

    def right_product(arrived):
        product = dot(arrived, right_table[0]) + dot(arrived, right_table[1])
        real = product[:step, :side] - product[step:, side:]
        imag = product[:step, side:] + product[step:, :side]
        return real, imag

    def put_gradient(job, gradient):
        for c in range(2):
            grads[job, c] = gradient[c].astype(BF16)

    def window_of(job):
        return pl.ds(unit_of(job) % chunks * step, step)

    def keeps(job):
        return block == unit_of(job) // chunks

    def gives(job):
        return block != unit_of(job) // chunks

    def strip(job, which, c, near):
        sources = [(grads, masks.at[0]), (grads_in, masks.at[1])]
        total = None
        for value, mask in sources:
            term = value[job, c].astype(F32) * mask[which, unit_of(job)].astype(F32)
            total = term if total is None else total + term
        for place in range(2 if near else 0):
            mask = near_masks[place, which, unit_of(job) % chunks].astype(F32)
            total = total + near_in[place, job, c].astype(F32) * mask
        return total

    def keep_strips(job, near):
        for c in range(2):
            mid_out[job, c] = strip(job, 1 - half, c, near).astype(BF16)
        mid_copy(job).start()
        for c in range(2):
            value = strip(job, half, c, near)
            if job < units:
                out[c, 0, window_of(job), :] = value
            else:
                own_out[job - units, c] = value.astype(BF16)
        if job >= units:
            own_copy(job).start()

    def stage_sum(job):
        @pl.when(keeps(job))
        def _():
            tile_copy(job).wait_recv()
            pass_copy(job).wait_recv()
            keep_strips(job, True)

    def stage_wide(job):
        @pl.when(keeps(job))
        def _():
            tile_copy(job).wait_recv()
            near_copy(job, False).wait_recv()
            wide_copy(job).wait_recv()
            keep_strips(job, True)

    def stage_direct(job):
        tile_copy(job).wait_recv()

        @pl.when(gives(job))
        def _():
            for c in range(2):
                far_out[job, c] = strip(job, 1 - half, c, False).astype(BF16)
            far_copy(job).start()
            for c in range(2):
                near_out[job, c] = strip(job, half, c, False).astype(BF16)
            near_copy(job, True).start()

        @pl.when(keeps(job))
        def _():
            keep_strips(job, False)

    def stage_pass(job):
        @pl.when(keeps(job))
        def _():
            near_copy(job, False).wait_recv()
            pass_copy(job).start()

    def stage_add(job, direct):
        @pl.when(keeps(job))
        def _():
            if job < units:
                first = [out[c, 0, window_of(job), :] for c in range(2)]
            else:
                own_copy(job).wait_recv()
                first = [own_in[job - units, c].astype(F32) for c in range(2)]
            if direct:
                near_copy(job, True).wait_recv()
                far_copy(job).wait_recv()
            mid_copy(job).wait_recv()
            for c in range(2):
                total = first[c] + mid_in[job, c].astype(F32)
                if direct:
                    total = total + near_in[0, job, c].astype(F32) + far_in[job, c].astype(F32)
                out[c, 0, window_of(job), :] = total

    def stage_masks(place):
        if place > 0:
            corner_copy(place).wait_recv()
        if place < 2:
            make_masks(masks, place, units, 0)
        else:
            make_masks(near_masks, place, chunks, block * rows)

    def send(job, mode):
        if mode == "d":
            tile_copy(job).start()
        else:

            @pl.when(keeps(job))
            def _():
                tile_copy(job).start()

            @pl.when(gives(job))
            def _():
                near_copy(job, False).start()
                if mode == "w":
                    wide_copy(job).start()

    def finish(jobs, modes):
        for half_units in range(2):
            count = dict.fromkeys(kinds, 0)
            for job in jobs:
                own_half = unit_of(job) // chunks == half_units
                mode = modes[job]
                count["tile"] += own_half or mode == "d"
                count["mid"] += own_half
                count["own"] += own_half and job >= units
                count["near"] += not own_half
                count["aux"] += mode == "r" if own_half else mode != "r"

            @pl.when(block == half_units)
            def _():
                wait_sent("tile", grads, count["tile"])
                wait_sent("near", grads, count["near"])
                wait_sent("aux", grads, count["aux"])
                wait_sent("mid", mid_out, count["mid"])
                wait_sent("own", own_out, count["own"])

    def run(order, modes, jobs, stage_gradient):
        stages = dict(
            g=stage_gradient,
            m=stage_masks,
            d=stage_direct,
            p=stage_pass,
            s=stage_sum,
            w=stage_wide,
            a=lambda job: stage_add(job, (top_modes if job >= units else modes)[job] == "d"),
        )
        for kind, number in order:
            stages[kind](number)
        wait_sent("corner", corners, 3)
        finish(jobs, modes)

    @pl.when(is_top)
    def _():
        fill_corners()
        load_table.wait()
        for part in range(2):
            product = dot(row_move, table[part]).astype(BF16)
            for unit in range(units):
                for c in range(2):
                    left_table[unit, 2 * part + c] = product[
                        unit * step : (unit + 1) * step, c * side : (c + 1) * side
                    ]
        load_residual.wait()
        load_layers.wait()
        handed = conj_times(
            layers[0, 0, 0].astype(F32), layers[0, 0, 1].astype(F32), residual[0, 0], residual[0, 1]
        )
        handed = jnp.concatenate([handed[0].astype(BF16), handed[1].astype(BF16)], axis=1)
        first = True
        for unit in [number for kind, number in bottom_order if kind == "g"] + list(kept):
            product = dot(left_table[unit].reshape(4 * step, side), handed)
            by_real = product[:step] + product[2 * step : 3 * step]
            by_imag = product[step : 2 * step] + product[3 * step :]
            hand_out[unit, 0] = (by_real[:, :side] - by_imag[:, side:]).astype(BF16)
            hand_out[unit, 1] = (by_real[:, side:] + by_imag[:, :side]).astype(BF16)
            if first:
                wait_depth()
                first = False
            if unit not in kept:
                hand_copy(unit).start()
        corner_copy(1).start()
        load_waves.wait()
        gradient = conj_times(
            waves[0, 0, 0].astype(F32), waves[0, 0, 1].astype(F32), residual[0, 0], residual[0, 1]
        )
        gradient = [roll(gradient[c].astype(BF16)) for c in range(2)]
        for unit in range(units):
            put_gradient(unit, [gradient[c][unit * step : (unit + 1) * step] for c in range(2)])
        wait_probe(13)
        corner_copy(2).start()
        corner_copy(3).start()

        def stage_gradient(job):
            if job == units:
                roll_right_table()
            if job >= units:
                real, imag = right_product(hand_out[unit_of(job)].reshape(2 * step, side))
                rolled_copy(job - units).wait_recv()
                source = rolled_in[job - units].astype(F32)
                put_gradient(job, conj_times(source[0], source[1], real, imag))
            send(job, top_modes[job])

        run(top_order, top_modes, range(units + len(kept)), stage_gradient)
        wait_sent("hand", hand_out, units - len(kept))

    @pl.when(is_bottom)
    def _():
        fill_corners()
        load_waves.wait()
        source = [roll(waves[0, 0, c]) for c in range(2)]
        for unit in range(units):
            for c in range(2):
                rolled[unit, c] = source[c][unit * step : (unit + 1) * step]
        wait_depth()
        for place in range(len(kept)):
            rolled_copy(place).start()
        corner_copy(1).start()
        load_table.wait()
        roll_right_table()
        wait_probe(7)
        corner_copy(2).start()
        corner_copy(3).start()

        def stage_gradient(job):
            hand_copy(job).wait_recv()
            real, imag = right_product(hand_in[job].reshape(2 * step, side))
            source = rolled[job].astype(F32)
            put_gradient(job, conj_times(source[0], source[1], real, imag))
            send(job, bottom_modes[job])

        jobs = [unit for unit in range(units) if unit not in kept]
        run(bottom_order, bottom_modes, jobs, stage_gradient)
        wait_sent("rolled", rolled, len(kept))


def orders(text):
    return [(step[0], int(step[1:])) for step in text]


def rolled_call(waves, layers, residual, offsets, slot, rows, columns, step, kept, top, bottom):
    side = waves.shape[-1]
    table = propagator(side)
    units = side // step
    jobs = units + len(kept)
    hbm = pl.BlockSpec(memory_space=pltpu.HBM)

    def copies(count):
        return pltpu.SemaphoreType.DMA((count,))

    return pl.pallas_call(
        functools.partial(rolled_kernel, kept, top, bottom, orders(TOP_STEPS), orders(BOTTOM_STEPS)),
        out_shape=jax.ShapeDtypeStruct((2, 1, rows, columns), F32),
        in_specs=[hbm] * 4 + [pl.BlockSpec(memory_space=pltpu.SMEM), hbm],
        out_specs=pl.BlockSpec(memory_space=pltpu.VMEM),
        scratch_shapes=[
            pltpu.VMEM(waves.shape, waves.dtype),
            pltpu.VMEM(layers.shape, layers.dtype),
            pltpu.VMEM(residual.shape, residual.dtype),
            pltpu.VMEM(table.shape, BF16),
            pltpu.SMEM(offsets.shape[::-1], jnp.int32),
            pltpu.VMEM((units, 4, step, side), BF16),
            pltpu.VMEM(table.shape, BF16),
            pltpu.VMEM((units, 2, step, side), BF16),
            pltpu.VMEM((units, 2, step, side), BF16),
            pltpu.VMEM((units, 2, step, side), BF16),
            pltpu.VMEM((max(len(kept), 1), 2, step, side), BF16),
            pltpu.VMEM((jobs, 2, step, side), BF16),
            pltpu.VMEM((jobs, 2, step, side), BF16),
            pltpu.VMEM((2, jobs, 2, step, side), BF16),
            pltpu.VMEM((jobs, 2, step, side), BF16),
            pltpu.VMEM((jobs, 2, step, side), BF16),
            pltpu.VMEM((jobs, 2, step, side), BF16),
            pltpu.VMEM((2, 2, units, step, side), BF16),
            pltpu.VMEM((2, 2, rows // step, step, side), BF16),
            pltpu.VMEM((4, 16, side), jnp.int32),
            pltpu.VMEM((jobs, 2, step, columns), BF16),
            pltpu.VMEM((jobs, 2, step, columns), BF16),
            pltpu.VMEM((max(len(kept), 1), 2, step, columns), BF16),
            pltpu.VMEM((max(len(kept), 1), 2, step, columns), BF16),
            pltpu.SemaphoreType.DMA((5,)),
            copies(8),
            copies(units),
            copies(max(len(kept), 1)),
            copies(3),
            copies(jobs),
            copies(rows // step + len(kept)),
            copies(rows // step + len(kept)),
            copies(rows // step + len(kept)),
            copies(max(len(kept), 1)),
            pltpu.SemaphoreType.REGULAR((2,)),
        ],
        compiler_params=pltpu.CompilerParams(
            collective_id=0, has_side_effects=True, vmem_limit_bytes=32 * 1024 * 1024
        ),
    )(
        *(pltpu.with_memory_space_constraint(x, pltpu.HBM) for x in (waves, layers, residual, offsets.T)),
        slot,
        pltpu.with_memory_space_constraint(jnp.asarray(table), pltpu.HBM),
    )


def per_device(depth_count, probe_count, tile_count, waves, layers, residual, offsets, slot):
    side = waves.shape[-1]
    rows, columns = OBJ // probe_count, OBJ // tile_count
    if (depth_count, probe_count, tile_count) == (2, 4, 2) and OBJ == 2 * side:
        return rolled_call(
            waves, layers, residual, offsets, slot, rows, columns, 32, KEPT, TOP_MODES, BOTTOM_MODES
        )
    table = propagator(side)
    others = probe_count // 2 - 1
    vmem = pl.BlockSpec(memory_space=pltpu.VMEM)
    smem = pl.BlockSpec(memory_space=pltpu.SMEM)
    hbm = pl.BlockSpec(memory_space=pltpu.HBM)
    return pl.pallas_call(
        functools.partial(kernel, depth_count, probe_count),
        out_shape=jax.ShapeDtypeStruct((2, 1, rows, columns), F32),
        in_specs=[hbm, hbm, hbm, smem, smem, hbm],
        out_specs=vmem,
        scratch_shapes=[
            pltpu.VMEM(waves.shape, waves.dtype),
            pltpu.VMEM(layers.shape, layers.dtype),
            pltpu.VMEM(residual.shape, residual.dtype),
            pltpu.VMEM(table.shape, BF16),
            pltpu.VMEM((2, side, side), BF16),
            pltpu.VMEM((2, side, side), BF16),
            pltpu.VMEM((side, 2 * side), BF16),
            pltpu.VMEM((2, 2, side, side), BF16),
            pltpu.VMEM((2, 16, side), jnp.int32),
            pltpu.VMEM((probe_count, rows, columns), BF16),
            pltpu.VMEM((probe_count, rows, columns), BF16),
            pltpu.VMEM((others, rows, columns), BF16),
            pltpu.VMEM((others, rows, columns), BF16),
            pltpu.VMEM((others, rows, columns), BF16),
            pltpu.VMEM((others, rows, columns), BF16),
            pltpu.VMEM((others, rows, columns), F32),
            pltpu.SemaphoreType.DMA((4,)),
            pltpu.SemaphoreType.DMA((2, CHUNKS)),
            pltpu.SemaphoreType.DMA((2, CHUNKS)),
            pltpu.SemaphoreType.DMA((2,)),
            pltpu.SemaphoreType.DMA((2, probe_count)),
            pltpu.SemaphoreType.DMA((2, others)),
            pltpu.SemaphoreType.DMA((2, others)),
        ],
        compiler_params=pltpu.CompilerParams(
            collective_id=0, has_side_effects=True, vmem_limit_bytes=32 * 1024 * 1024
        ),
    )(
        *(pltpu.with_memory_space_constraint(x, pltpu.HBM) for x in (waves, layers, residual)),
        offsets.T,
        slot,
        pltpu.with_memory_space_constraint(jnp.asarray(table), pltpu.HBM),
    )


def solution(mesh):
    return jax.shard_map(
        functools.partial(per_device, mesh.shape["depth"], mesh.shape["probe"], mesh.shape["tile"]),
        mesh=mesh,
        in_specs=(
            P("depth", ("groups", "probe", "tile"), None, None, None),
            P("depth", ("groups", "probe", "tile"), None, None, None),
            P(("groups", "probe", "tile"), None, None, None),
            P("groups", None),
            P(("groups", "probe", "tile")),
        ),
        out_specs=P("groups", "depth", "probe", "tile"),
        check_vma=False,
    )
```
